256 devices in a mesh: src: 32 (over z, x), dst: 8 (over y, core).
Axes of the slice: x: 4, y: 4, z: 8, core: 2. Of those that a mesh axis runs over, the one named last changes fastest.
Arguments:
- counts: int32 [8, 8192, 8192], P(None, 'src', 'dst'), may hold values from 0 to 63
- src_factor: float32 [8192, 128], P('src'), may hold values from 0.25 to 32
- dst_factor: float32 [8192, 128], P('dst'), may hold values from 0.25 to 32
- hour_factor: float32 [8, 32], replicated, may hold values from 0.25 to 4
- core: float32 [32, 128, 128], replicated, may hold values from 1e-06 to 1e-05
Outputs:
- grad_src: float32 [8192, 128], P('src')
- grad_dst: float32 [8192, 128], P('dst')
- grad_hour: float32 [8, 32], replicated
- grad_core: float32 [32, 128, 128], P(None, 'src')
The draws below stay inside these ranges and needn't reach their ends.
All inputs are finite; a program needn't handle non-finite values.
Results may differ from the reference program's by a relative error of at most 0.0003.
Values sent between devices are 32-bit elements; how exact they have to be, the bound alone decides.
No kernel may reach another device: no remote copies, remote signals or barrier semaphores. Data moves between devices by JAX's collectives and lax.ppermute only.
A program may use at most 64 MiB of HBM per device.

```python
import math
import jax
import jax.numpy as jnp
from jax import lax

HOURS = 8
R1 = 128
R2 = 128
R3 = 32
I = 8192
J = 8192
N_SRC = 32


def row_groups(key, salt, number):
    return jax.random.randint(jax.random.fold_in(key, salt), (number,), 0, 8).astype(jnp.int32)


def boosted(base, groups, width):
    columns = jnp.arange(width, dtype=jnp.int32) % 8
    boost = jnp.where(columns[None, :] == groups[:, None], 8.0, 1.0).astype(jnp.float32)
    return (base * boost).astype(jnp.float32)


def draw_counts(key, part):
    src_groups = row_groups(key, 11, I)
    dst_groups = row_groups(key, 12, J)
    levels = jax.random.randint(jax.random.fold_in(key, 13), (8, 8), 12, 65).astype(jnp.int32)
    src_levels = jnp.take(levels, src_groups, axis=0)
    pair_level = jnp.take(src_levels, dst_groups, axis=1)
    raw_counts = jax.random.randint(jax.random.fold_in(key, 14), (HOURS, I, J), 0, 64).astype(jnp.int32)
    return jnp.minimum(raw_counts * pair_level[None, :, :] // 48, 63).astype(jnp.int32)


def draw_src_factor(key, part):
    groups = row_groups(key, 11, I)
    sub_key = jax.random.fold_in(key, 21)
    base = jnp.exp(jax.random.uniform(sub_key, (I, R1), jnp.float32, jnp.log(0.25), jnp.log(4.0)))
    return boosted(base, groups, R1)


def draw_dst_factor(key, part):
    groups = row_groups(key, 12, J)
    sub_key = jax.random.fold_in(key, 22)
    base = jnp.exp(jax.random.uniform(sub_key, (J, R2), jnp.float32, jnp.log(0.25), jnp.log(4.0)))
    return boosted(base, groups, R2)


def setup_inputs(seed: int = 0) -> dict:
    keys = jax.random.split(jax.random.key(seed), 6)
    return {
        "counts": draw_counts(jax.random.fold_in(keys[5], 71), 0),
        "src_factor": draw_src_factor(jax.random.fold_in(keys[5], 71), 0),
        "dst_factor": draw_dst_factor(jax.random.fold_in(keys[5], 71), 0),
        "hour_factor": jnp.clip(jnp.exp(jax.random.uniform(keys[3], (HOURS, R3), jnp.float32, math.log(0.25), math.log(4.0))), 0.25, 4.0),
        "core": jnp.clip(jnp.exp(jax.random.uniform(keys[4], (R3, R1, R2), jnp.float32, math.log(9.999999974752427e-07), math.log(9.999999747378752e-06))), 9.999999974752427e-07, 9.999999747378752e-06),
    }


def reference(counts, src_factor, dst_factor, hour_factor, core):
    highest = lax.Precision.HIGHEST
    core_hours = jnp.einsum('kr,rpq->kpq', hour_factor, core, precision=highest)
    row_count = I // N_SRC

    def block_step(totals, block_index):
        offset = (block_index * row_count).astype(jnp.int32)
        block_counts = lax.dynamic_slice_in_dim(counts, offset, row_count, 1).astype(jnp.float32)
        block_src = lax.dynamic_slice_in_dim(src_factor, offset, row_count, 0)
        partial_fit = jnp.einsum('ip,kpq->kiq', block_src, core_hours, precision=highest)
        fitted = jnp.einsum('kiq,jq->kij', partial_fit, dst_factor, precision=highest)
        misfit = 1.0 - block_counts / fitted
        dst_sum = totals[0] + jnp.einsum('kij,kiq->jq', misfit, partial_fit, precision=highest)
        through = jnp.einsum('kij,jq->kiq', misfit, dst_factor, precision=highest)
        src_block = jnp.einsum('kiq,kpq->ip', through, core_hours, precision=highest)
        projected = totals[1] + jnp.einsum('ip,kiq->kpq', block_src, through, precision=highest)
        return ((dst_sum, projected), src_block)
    start_totals = (jnp.zeros((J, R2), jnp.float32), jnp.zeros((HOURS, R1, R2), jnp.float32))
    (dst_sum, projected), src_blocks = lax.scan(block_step, start_totals, jnp.arange(N_SRC, dtype=jnp.int32))
    grad_src = src_blocks.reshape(I, R1) / math.sqrt(J * HOURS)
    grad_dst = dst_sum / math.sqrt(I * HOURS)
    grad_hour = jnp.einsum('kpq,rpq->kr', projected, core, precision=highest) / math.sqrt(I * J)
    grad_core = jnp.einsum('kr,kpq->rpq', hour_factor, projected, precision=highest) / math.sqrt(I * J * HOURS)
    return (grad_src, grad_dst, grad_hour, grad_core)
```

```python
import functools
import math

import jax
import jax.numpy as jnp
from jax import lax
from jax.experimental import pallas as pl
from jax.experimental.pallas import tpu as pltpu
from jax.sharding import Mesh, PartitionSpec as P

X = 4
CORES = 2
F32 = jnp.float32
BF16 = jnp.bfloat16


def split(x):
    hi = x.astype(BF16)
    return hi, (x - hi.astype(F32)).astype(BF16)


def mm(a, b):
    return jnp.dot(a, b, preferred_element_type=F32)


def halves(x, axis):
    hi, lo = split(x)
    return jnp.concatenate([hi, lo], axis=axis)


def quarters(x):
    row = halves(x, 1)
    return jnp.concatenate([row, row], axis=0)


def vmem(*shape):
    return pl.BlockSpec(shape, lambda *_: (0,) * len(shape))


def main_kernel(hour_ref, counts_ref, src_ref, dst_ref, core_ref,
                a0, a1, a2, a3, own, send,
                dst_cols, dst_rows, src_cols, src_rows, dst_sum, src_sum):
    k = pl.program_id(0)
    last = pl.num_programs(0) - 1
    hours = pl.num_programs(0)
    x, y, c = lax.axis_index("x"), lax.axis_index("y"), lax.axis_index("core")
    rank = core_ref.shape[0]
    rows, cols = counts_ref.shape[1], counts_ref.shape[2]
    p1, q1 = core_ref.shape[1], core_ref.shape[2]
    y_count = own.shape[0]

    @pl.when(k == 0)
    def _():
        dst = dst_ref[...]
        dst_rows[...] = halves(dst, 1)
        turned = dst.T
        hi, lo = split(turned)
        dst_cols[...] = jnp.concatenate([hi, hi, lo, lo], axis=0)
        src = src_ref[...]
        src_rows[...] = halves(src, 1)
        src_cols[...] = halves(src.T, 0)
        dst_sum[...] = jnp.zeros_like(dst_sum)
        src_sum[...] = jnp.zeros_like(src_sum)

    core_hour = hour_ref[k, 0] * core_ref[0]
    for r in range(1, rank):
        core_hour = core_hour + hour_ref[k, r] * core_ref[r]

    both = mm(src_rows[...], quarters(core_hour))
    fit = both[:, :q1] + both[:, q1:]
    fit_rows = halves(fit, 1)
    fit_rows = jnp.concatenate([fit_rows, fit_rows], axis=1)
    fit_cols = halves(fit.T, 0)

    through = jnp.zeros((rows, q1), F32)
    step = 256
    for j in range(0, cols, step):
        fitted = mm(fit_rows, dst_cols[:, j:j + step])
        misfit = 1.0 - counts_ref[0, :, j:j + step].astype(F32) / fitted
        hi, lo = split(misfit)
        both = mm(jnp.concatenate([hi, lo], axis=0), dst_rows[j:j + step, :])
        both = both[:rows] + both[rows:]
        through = through + (both[:, :q1] + both[:, q1:])
        first = mm(fit_cols, hi)
        second = mm(fit_cols[:q1], lo)
        dst_sum[:, j:j + step] += first[:q1] + (first[q1:] + second)

    turned = core_hour.T
    th = halves(through, 1)
    both = mm(th, quarters(turned))
    src_sum[...] += both[:, :p1] + both[:, p1:]
    both = mm(src_cols[...], th)
    both = both[:p1] + both[p1:]
    projected = both[:, :q1] + both[:, q1:]
    slot = lax.rem(k // CORES - y + y_count, y_count)

    @pl.when(lax.rem(k, CORES) == c)
    def _():
        own[slot, :p1, :] = projected

    @pl.when(lax.rem(k, CORES) != c)
    def _():
        send[slot, :p1, :] = projected

    @pl.when(k == last)
    def _():
        turned = dst_sum[...].T
        dst_rows_out = turned
        block = cols // X
        share = rows // hours
        for s, out in enumerate((a0, a1, a2, a3)):
            place = lax.rem(x + s, X)
            for b in range(X):
                @pl.when(place == b)
                def _():
                    out[...] = dst_rows_out[b * block:(b + 1) * block]
        for s in range(y_count):
            other = lax.rem(y + s, y_count) * CORES
            own[s, p1:, :] = src_sum[pl.ds(pl.multiple_of((other + c) * share, share), share), :]
            send[s, p1:, :] = src_sum[pl.ds(pl.multiple_of((other + 1 - c) * share, share), share), :]


def main_call(counts, src, dst, hour, core):
    hours, rows, cols = counts.shape
    p1, q1 = core.shape[1:]
    block = cols // X
    share = rows // hours
    ys = hours // CORES
    out = [jax.ShapeDtypeStruct((block, q1), F32)] * X + [jax.ShapeDtypeStruct((ys, p1 + share, q1), F32)] * 2
    flops = 2 * 6 * hours * rows * cols * q1
    return pl.pallas_call(
        main_kernel,
        out_shape=out,
        grid=(hours,),
        in_specs=[
            pl.BlockSpec(memory_space=pltpu.SMEM),
            pl.BlockSpec((1, rows, cols), lambda k: (k, 0, 0)),
            vmem(rows, p1), vmem(cols, q1), vmem(*core.shape),
        ],
        out_specs=[vmem(block, q1)] * X + [vmem(ys, p1 + share, q1)] * 2,
        scratch_shapes=[
            pltpu.VMEM((4 * q1, cols), BF16),
            pltpu.VMEM((cols, 2 * q1), BF16),
            pltpu.VMEM((2 * p1, rows), BF16),
            pltpu.VMEM((rows, 2 * p1), BF16),
            pltpu.VMEM((q1, cols), F32),
            pltpu.VMEM((rows, p1), F32),
        ],
        compiler_params=pltpu.CompilerParams(vmem_limit_bytes=40 << 20),
        cost_estimate=pl.CostEstimate(flops=flops, bytes_accessed=12 << 20, transcendentals=0),
        name="gradient_terms",
    )(hour, counts, src, dst, core)


def add_kernel(own, came, *outs):
    for s, out in enumerate(outs):
        out[...] = own[s] + came[s]


def add_call(own, came):
    shape = own.shape[1:]
    return pl.pallas_call(
        add_kernel,
        out_shape=[jax.ShapeDtypeStruct(shape, F32)] * own.shape[0],
        name="core_sum",
    )(own, came)


def share_kernel(t0, r1, r2, r3, core_ref, m0, m1, m2, m3, src_out):
    x = lax.axis_index("x")
    total = (t0[...] + r1[...]) + (r2[...] + r3[...])
    p1 = core_ref.shape[1]
    rank = core_ref.shape[0]
    src_out[...] = total[p1:]
    projected = total[:p1]
    lanes = lax.broadcasted_iota(jnp.int32, (8, 128), 1)
    hour = jnp.zeros((8, 128), F32)
    for r in range(rank):
        prod = projected * core_ref[r]
        part = jnp.sum(prod, axis=0, keepdims=True)
        value = jnp.sum(part, axis=1, keepdims=True)
        hour = jnp.where(lanes == r, value, hour)
    tiles = projected.reshape(p1 // 16, X, 4, 128)
    for s, out in enumerate((m0, m1, m2, m3)):
        place = lax.rem(x + s, X)
        for b in range(X):
            @pl.when(place == b)
            def _():
                for z in range(p1 // 16):
                    out[4 * z:4 * z + 4, :] = tiles[z, b]
        out[p1 // 4:, :] = hour


def share_call(t0, r1, r2, r3, core):
    rows, q1 = t0.shape
    p1 = core.shape[1]
    out = [jax.ShapeDtypeStruct((p1 // 4 + 8, q1), F32)] * X + [jax.ShapeDtypeStruct((rows - p1, q1), F32)]
    return pl.pallas_call(share_kernel, out_shape=out, name="hour_terms")(t0, r1, r2, r3, core)


def z_kernel(a_ref, m0, m1, m2, m3, out):
    zs, share, _ = a_ref.shape
    total = jnp.sum(a_ref[...], axis=0)
    m = (m0[...] + m1[...]) + (m2[...] + m3[...])
    for z in range(zs):
        out[z, :share, :] = total
        out[z, share:share + 4, :] = m[4 * z:4 * z + 4]
        out[z, share + 4:, :] = m[4 * zs:4 * zs + 4]


def z_call(a, m):
    zs, share, q1 = a.shape
    return pl.pallas_call(
        z_kernel, out_shape=jax.ShapeDtypeStruct((zs, share + 8, q1), F32), name="z_terms",
    )(a, *m)


def back_kernel(w, src_part, block, rest):
    zs, rows, _ = w.shape
    share = rows - 8
    tail = w[0, share:, :]
    block[:share, :] = w[0, :share, :]
    for z in range(1, zs):
        block[z * share:(z + 1) * share, :] = w[z, :share, :]
        tail = tail + w[z, share:, :]
    rest[:8, :] = tail
    rest[8:, :] = src_part[...]


def back_call(w, src_part):
    zs, rows, q1 = w.shape
    return pl.pallas_call(
        back_kernel,
        out_shape=[jax.ShapeDtypeStruct((zs * (rows - 8), q1), F32),
                   jax.ShapeDtypeStruct((src_part.shape[0] + 8, q1), F32)],
        name="z_sums",
    )(w, src_part)


def pair_kernel(own, other, out):
    c = lax.axis_index("core")
    out[c] = own[...]
    out[1 - c] = other[...]


def pair_call(own, other):
    return pl.pallas_call(
        pair_kernel, out_shape=jax.ShapeDtypeStruct((2, *own.shape), F32), name="core_pair",
    )(own, other)


def end_kernel(scales, hour_ref, b0, b1, b2, b3, d0, d1, d2, d3, src_out, dst_out, hour_out, core_out, shares):
    x, y = lax.axis_index("x"), lax.axis_index("y")
    src_scale, dst_scale, hour_scale, core_scale = scales
    for s, block in enumerate((b0, b1, b2, b3)):
        dst_out[lax.rem(x - s + X, X)] = block[...] * dst_scale
    for s, pair in enumerate((d0, d1, d2, d3)):
        spot = lax.rem(y - s + 4, 4)
        for c in range(CORES):
            at = spot * CORES + c
            shares[at] = pair[c, :8, :]
            src_out[at] = pair[c, 8:, :] * src_scale
    hours, rank = hour_ref.shape
    for k in range(hours):
        hour_out[k:k + 1, :] = shares[k, 4:5, :rank] * hour_scale
    tiles = [shares[k, :4, :] * core_scale for k in range(hours)]
    for r in range(rank):
        total = hour_ref[0, r] * tiles[0]
        for k in range(1, hours):
            total = total + hour_ref[k, r] * tiles[k]
        core_out[r] = total


def end_call(scales, hour, blocks, pairs):
    block, q1 = blocks[0].shape
    share = pairs[0].shape[1] - 8
    hours, rank = hour.shape
    whole = pl.BlockSpec(memory_space=pltpu.VMEM)
    return pl.pallas_call(
        functools.partial(end_kernel, scales),
        in_specs=[pl.BlockSpec(memory_space=pltpu.SMEM)] + [whole] * 8,
        out_specs=[whole] * 4,
        out_shape=[jax.ShapeDtypeStruct((hours, share, q1), F32),
                   jax.ShapeDtypeStruct((X, block, q1), F32),
                   jax.ShapeDtypeStruct((hours, rank), F32),
                   jax.ShapeDtypeStruct((rank, 4, q1), F32)],
        scratch_shapes=[pltpu.VMEM((hours, 8, q1), F32)],
        name="outputs",
    )(hour, *blocks, *pairs)


def shifted(x, axis, s):
    n = lax.axis_size(axis)
    return lax.ppermute(x, axis, [(i, (i + s) % n) for i in range(n)])


def swapped(x, axis):
    n = lax.axis_size(axis)
    return lax.all_to_all(x, axis, split_axis=0, concat_axis=0, tiled=True)


def shards(scales, counts, src_factor, dst_factor, hour_factor, core):
    z_count = lax.axis_size("z")
    a0, a1, a2, a3, own, send = main_call(counts, src_factor, dst_factor, hour_factor, core)
    came = [shifted(a, "x", s) for s, a in ((1, a1), (2, a2), (3, a3))]
    other = shifted(send, "core", 1)
    parts = add_call(own, other)
    y_came = [shifted(parts[s], "y", s) for s in (1, 2, 3)]
    a = (a0 + came[0]) + (came[1] + came[2])
    a = swapped(a.reshape(z_count, -1, a.shape[-1]), "z")
    m0, m1, m2, m3, src_part = share_call(parts[0], *y_came, core)
    m = [m0] + [shifted(v, "x", s) for s, v in ((1, m1), (2, m2), (3, m3))]
    w = swapped(z_call(a, m), "z")
    block, rest = back_call(w, src_part)
    pair = pair_call(rest, shifted(rest, "core", 1))
    blocks = [block] + [shifted(block, "x", s) for s in (1, 2, 3)]
    pairs = [pair] + [shifted(pair, "y", s) for s in (1, 2, 3)]
    grad_src, grad_dst, grad_hour, grad_core = end_call(scales, hour_factor, blocks, pairs)
    return (grad_src.reshape(src_factor.shape), grad_dst.reshape(dst_factor.shape), grad_hour, grad_core)


def solution(mesh):
    n_src, n_dst = mesh.shape["src"], mesh.shape["dst"]
    fine = Mesh(mesh.devices.reshape(n_src // X, X, n_dst // CORES, CORES), ("z", "x", "y", "core"))
    src, dst = ("z", "x"), ("y", "core")
    in_specs = (P(None, src, dst), P(src, None), P(dst, None), P(), P())
    out_specs = (P(src, None), P(dst, None), P(), P(None, src, None))

    def run(counts, src_factor, dst_factor, hour_factor, core):
        hours, total_src, total_dst = counts.shape
        scales = (1 / math.sqrt(total_dst * hours), 1 / math.sqrt(total_src * hours),
                  1 / math.sqrt(total_src * total_dst), 1 / math.sqrt(total_src * total_dst * hours))
        body = jax.shard_map(functools.partial(shards, scales), mesh=fine, in_specs=in_specs,
                             out_specs=out_specs, check_vma=False)
        return body(counts, src_factor, dst_factor, hour_factor, core)

    return run
```

```python
import functools
import math

import jax
import jax.numpy as jnp
from jax import lax
from jax.experimental import pallas as pl
from jax.experimental.pallas import tpu as pltpu
from jax.sharding import Mesh, PartitionSpec as P

X = 4
CORES = 2
PAIR = 2
SPAN = 1024
F32 = jnp.float32
BF16 = jnp.bfloat16
ANY = pl.BlockSpec(memory_space=pl.ANY)
VMEM = pl.BlockSpec(memory_space=pltpu.VMEM)
SMEM = pl.BlockSpec(memory_space=pltpu.SMEM)


def struct(*shape, dtype=F32):
    return jax.ShapeDtypeStruct(shape, dtype)


def params(mib):
    return pltpu.CompilerParams(vmem_limit_bytes=mib << 20)


def cost(flops, size):
    return pl.CostEstimate(flops=flops, bytes_accessed=size, transcendentals=0)


def split(x):
    hi = x.astype(BF16)
    return hi, (x - hi.astype(F32)).astype(BF16)


def mm(a, b):
    return jnp.dot(a, b, preferred_element_type=F32)


def halves(x, axis):
    return jnp.concatenate(split(x), axis=axis)


def first_kernel(hour_ref, counts_hbm, src_hbm, dst_hbm, core_hbm,
                 a0, a1, a2, a3, hours_out, hi_hbm, lo_hbm,
                 counts, src, dst, core, fit_rows, fit_cols, dst_cols, hi_all, lo_all, dst_sum, turned, sems):
    hours, rows, cols = counts.shape
    rank, p1, q1 = core.shape
    steps = hours // PAIR
    x = lax.axis_index("x")
    small = [pltpu.make_async_copy(a, b, sems.at[i])
             for i, (a, b) in enumerate(((core_hbm, core), (src_hbm, src), (dst_hbm, dst)))]
    parts = [pl.ds(s * PAIR, PAIR) for s in range(steps)]
    large = [pltpu.make_async_copy(counts_hbm.at[part], counts.at[part], sems.at[3 + s])
             for s, part in enumerate(parts)]
    for copy in small + large:
        copy.start()
    small[2].wait()
    hi, lo = split(dst[...].T)
    dst_cols[...] = jnp.concatenate([hi, hi, lo], axis=0)
    small[0].wait()
    small[1].wait()
    hi, lo = split(src[...])
    src_rows = jnp.concatenate([hi, lo, hi], axis=1)
    for k in range(hours):
        core_hour = hour_ref[k, 0] * core[0]
        for r in range(1, rank):
            core_hour = core_hour + hour_ref[k, r] * core[r]
        hours_out[k] = core_hour
        hi, lo = split(core_hour)
        fit = mm(src_rows, jnp.concatenate([hi, hi, lo], axis=0))
        hi, lo = split(fit)
        fit_rows[k * rows:(k + 1) * rows] = jnp.concatenate([hi, lo, hi], axis=1)
        fit_cols[k] = halves(fit.T, 0)
    sends = []
    for s, part in enumerate(parts):
        large[s].wait()
        block = pl.ds(s * PAIR * rows, PAIR * rows)
        for j in range(0, cols, SPAN):
            wide = pl.ds(j, SPAN)
            fitted = mm(fit_rows[block, :], dst_cols[:, wide])
            misfit = 1.0 - counts[part, :, wide].reshape(PAIR * rows, SPAN).astype(F32) / fitted
            hi, lo = split(misfit)
            hi_all[part, :, wide] = hi.reshape(PAIR, rows, SPAN)
            lo_all[part, :, wide] = lo.reshape(PAIR, rows, SPAN)
            total = None
            for k in range(PAIR):
                left = fit_cols[s * PAIR + k]
                both = mm(left, hi[k * rows:(k + 1) * rows])
                term = both[:q1] + (both[q1:] + mm(left[:q1], lo[k * rows:(k + 1) * rows]))
                total = term if total is None else total + term
            if s == 0:
                dst_sum[:, wide] = total
            else:
                dst_sum[:, wide] += total
        for i, (a, b) in enumerate(((hi_all, hi_hbm), (lo_all, lo_hbm))):
            sends.append(pltpu.make_async_copy(a.at[part], b.at[part], sems.at[3 + steps + 2 * s + i]))
            sends[-1].start()
    turned[...] = dst_sum[...].T.reshape(turned.shape)
    for s, out in enumerate((a0, a1, a2, a3)):
        out[...] = turned[lax.rem(x + s, X)]
    for copy in sends:
        copy.wait()


def first_call(hour, counts, src, dst, core):
    hours, rows, cols = counts.shape
    rank, p1, q1 = core.shape
    block = cols // X
    out = [struct(block, q1)] * X + [struct(hours, p1, q1)] + [struct(*counts.shape, dtype=BF16)] * 2
    return pl.pallas_call(
        first_kernel,
        out_shape=out,
        in_specs=[SMEM] + [ANY] * 4,
        out_specs=[VMEM] * (X + 1) + [ANY] * 2,
        scratch_shapes=[
            pltpu.VMEM(counts.shape, jnp.int32),
            pltpu.VMEM(src.shape, F32),
            pltpu.VMEM(dst.shape, F32),
            pltpu.VMEM(core.shape, F32),
            pltpu.VMEM((hours * rows, 3 * q1), BF16),
            pltpu.VMEM((hours, 2 * q1, rows), BF16),
            pltpu.VMEM((3 * q1, cols), BF16),
            pltpu.VMEM(counts.shape, BF16),
            pltpu.VMEM(counts.shape, BF16),
            pltpu.VMEM((q1, cols), F32),
            pltpu.VMEM((X, block, q1), F32),
            pltpu.SemaphoreType.DMA((3 + 3 * (hours // PAIR),)),
        ],
        compiler_params=params(60),
        cost_estimate=cost(2 * 6 * counts.size * q1, 20 << 20),
        name="misfit_and_dst",
    )(hour, counts, src, dst, core)


def second_kernel(hi_hbm, lo_hbm, src_hbm, dst_hbm, core_hbm, hours_hbm,
                  m0, m1, m2, m3, src_own, src_send,
                  hi_all, lo_all, src, dst, core, core_hours, dst_rows, src_cols, projected, rowsums, message, src_all, sems):
    hours, rows, cols = hi_all.shape
    rank, p1, q1 = core.shape
    steps = hours // PAIR
    zs = message.shape[1]
    x = lax.axis_index("x")
    small = [pltpu.make_async_copy(a, b, sems.at[i])
             for i, (a, b) in enumerate(((dst_hbm, dst), (src_hbm, src), (hours_hbm, core_hours), (core_hbm, core)))]
    parts = [pl.ds(s * PAIR, PAIR) for s in range(steps)]
    large = []
    for s, part in enumerate(parts):
        for i, (a, b) in enumerate(((hi_hbm, hi_all), (lo_hbm, lo_all))):
            large.append(pltpu.make_async_copy(a.at[part], b.at[part], sems.at[4 + 2 * s + i]))
    for copy in small[:3] + large + small[3:]:
        copy.start()
    small[0].wait()
    dst_rows[...] = halves(dst[...], 1)
    small[1].wait()
    src_cols[...] = halves(src[...].T, 0)
    small[2].wait()
    src_sum = None
    for s, part in enumerate(parts):
        large[2 * s].wait()
        large[2 * s + 1].wait()
        both = mm(hi_all[part].reshape(PAIR * rows, cols), dst_rows[...])
        through = both[:, :q1] + (both[:, q1:] + mm(lo_all[part].reshape(PAIR * rows, cols), dst_rows[:, :q1]))
        for i in range(PAIR):
            k = s * PAIR + i
            th = halves(through[i * rows:(i + 1) * rows], 1)
            right = halves(core_hours[k].T, 1)
            both = mm(th, jnp.concatenate([right, right], axis=0))
            both = both[:, :p1] + both[:, p1:]
            src_sum = both if src_sum is None else src_sum + both
            both = mm(src_cols[...], th)
            both = both[:p1] + both[p1:]
            projected[k] = both[:, :q1] + both[:, q1:]
    y, c = lax.axis_index("y"), lax.axis_index("core")
    ys, share, _ = src_own.shape
    src_all[...] = src_sum.reshape(src_all.shape)
    for s in range(ys):
        at = lax.rem(y + s, ys) * CORES
        src_own[s] = src_all[at + c]
        src_send[s] = src_all[at + 1 - c]
    small[3].wait()
    for k in range(hours):
        here = projected[k]
        for r in range(rank):
            product = (here * core[r]).reshape(p1 // 8, 8, q1)
            at = k * rank + r
            rowsums[at:at + 1, :] = jnp.sum(jnp.sum(product, axis=0), axis=0, keepdims=True)
        for z in range(zs):
            for b in range(X):
                start = (z * X + b) * 4
                message[b, z, 4 * k:4 * k + 4, :] = here[start:start + 4]
    sums = jnp.sum(rowsums[...].T, axis=0, keepdims=True)
    spare = jnp.zeros((8 - sums.shape[1] // 128, 128), F32)
    tail = jnp.concatenate([sums[:, i:i + 128] for i in range(0, sums.shape[1], 128)] + [spare], axis=0)
    for s, out in enumerate((m0, m1, m2, m3)):
        out[:zs] = message[lax.rem(x + s, X)]
        out[zs, :8, :] = tail


def second_call(hi, lo, src, dst, core, core_hours, zs, devices):
    hours, rows, cols = hi.shape
    rank, p1, q1 = core.shape
    share = hours * p1 // (zs * X)
    return pl.pallas_call(
        second_kernel,
        out_shape=[struct(zs + 1, share, q1)] * X + [struct(devices // CORES, rows // devices, p1)] * 2,
        in_specs=[ANY] * 6,
        out_specs=[VMEM] * (X + 2),
        scratch_shapes=[
            pltpu.VMEM(hi.shape, BF16),
            pltpu.VMEM(hi.shape, BF16),
            pltpu.VMEM(src.shape, F32),
            pltpu.VMEM(dst.shape, F32),
            pltpu.VMEM(core.shape, F32),
            pltpu.VMEM(core_hours.shape, F32),
            pltpu.VMEM((cols, 2 * q1), BF16),
            pltpu.VMEM((2 * p1, rows), BF16),
            pltpu.VMEM((hours, p1, q1), F32),
            pltpu.VMEM((hours * rank, q1), F32),
            pltpu.VMEM((X, zs, share, q1), F32),
            pltpu.VMEM((devices, rows // devices, p1), F32),
            pltpu.SemaphoreType.DMA((4 + 2 * (hours // PAIR),)),
        ],
        compiler_params=params(60),
        cost_estimate=cost(2 * 3 * hi.size * q1, 12 << 20),
        name="src_and_projected",
    )(hi, lo, src, dst, core, core_hours)


def z_kernel(a, m0, m1, m2, m3, out):
    zs, share, _ = a.shape
    total = jnp.sum(a[...], axis=0)
    m = (m0[...] + m1[...]) + (m2[...] + m3[...])
    for z in range(zs):
        out[z, :share, :] = total
        out[z, share:2 * share, :] = m[z]
        out[z, 2 * share:, :] = m[zs, :8]


def z_call(a, m):
    zs, share, q1 = a.shape
    return pl.pallas_call(
        z_kernel, out_shape=struct(zs, 2 * share + 8, q1), in_specs=[VMEM] * 5, out_specs=VMEM,
        compiler_params=params(8), cost_estimate=cost(1 << 20, 1 << 20), name="z_terms",
    )(a, *m)


def pair_kernel(own, came, *outs):
    for s, out in enumerate(outs):
        out[...] = own[s] + came[s]


def pair_call(own, came):
    return pl.pallas_call(
        pair_kernel, out_shape=[struct(*own.shape[1:])] * own.shape[0],
        in_specs=[VMEM] * 2, out_specs=[VMEM] * own.shape[0],
        compiler_params=params(8), cost_estimate=cost(1 << 18, 1 << 18), name="core_sums",
    )(own, came)


def back_kernel(w, t0, t1, t2, t3, block, copies):
    zs, rows, _ = w.shape
    share = (rows - 8) // 2
    tail = w[0, share:, :]
    block[:share, :] = w[0, :share, :]
    for z in range(1, zs):
        block[z * share:(z + 1) * share, :] = w[z, :share, :]
        tail = tail + w[z, share:, :]
    total = (t0[...] + t1[...]) + (t2[...] + t3[...])
    for d in range(copies.shape[0]):
        copies[d, :share + 8, :] = tail
        copies[d, share + 8:, :] = total


def back_call(w, terms, devices):
    zs, rows, q1 = w.shape
    src_share = terms[0].shape[0]
    share = (rows - 8) // 2
    return pl.pallas_call(
        back_kernel, out_shape=[struct(zs * share, q1), struct(devices, rows - share + src_share, q1)],
        in_specs=[VMEM] * 5, out_specs=[VMEM] * 2,
        compiler_params=params(8), cost_estimate=cost(1 << 20, 1 << 20), name="z_sums",
    )(w, *terms)


def end_kernel(scales, hour_ref, b0, b1, b2, b3, d, src_out, dst_out, hour_out, core_out):
    x = lax.axis_index("x")
    src_scale, dst_scale, hour_scale, core_scale = scales
    for s, block in enumerate((b0, b1, b2, b3)):
        dst_out[lax.rem(x - s + X, X)] = block[...] * dst_scale
    hours, rank = hour_ref.shape
    share = 4 * hours
    total = jnp.sum(d[:, :share + 8, :], axis=0)
    src_out[...] = d[:, share + 8:, :] * src_scale
    each = 128 // rank
    for k in range(hours):
        row = share + k // each
        hour_out[k:k + 1, :] = total[row:row + 1, k % each * rank:(k % each + 1) * rank] * hour_scale
    tiles = [total[4 * k:4 * k + 4] * core_scale for k in range(hours)]
    for r in range(rank):
        out = hour_ref[0, r] * tiles[0]
        for k in range(1, hours):
            out = out + hour_ref[k, r] * tiles[k]
        core_out[r] = out


def end_call(scales, hour, blocks, d):
    block, q1 = blocks[0].shape
    hours, rank = hour.shape
    return pl.pallas_call(
        functools.partial(end_kernel, scales),
        in_specs=[SMEM] + [VMEM] * (X + 1),
        out_specs=[VMEM] * 4,
        out_shape=[struct(d.shape[0], d.shape[1] - 4 * hours - 8, q1), struct(X, block, q1), struct(hours, rank), struct(rank, 4, q1)],
        compiler_params=params(8), cost_estimate=cost(1 << 20, 1 << 20), name="outputs",
    )(hour, *blocks, d)


def shifted(x, axis, s):
    n = lax.axis_size(axis)
    return lax.ppermute(x, axis, [(i, (i + s) % n) for i in range(n)])


def swapped(x, axis):
    return lax.all_to_all(x, axis, split_axis=0, concat_axis=0, tiled=True)


def after(x, *others):
    return lax.optimization_barrier((x, *others))[0]


def shards(scales, counts, src_factor, dst_factor, hour_factor, core):
    zs = lax.axis_size("z")
    dst_axes = ("y", "core")
    devices = lax.axis_size(dst_axes)
    q1 = dst_factor.shape[1]
    a0, a1, a2, a3, core_hours, hi, lo = first_call(hour_factor, counts, src_factor, dst_factor, core)
    came = [shifted(a, "x", s) for s, a in ((1, a1), (2, a2), (3, a3))]
    m0, m1, m2, m3, src_own, src_send = second_call(
        hi, lo, src_factor, dst_factor, core, core_hours, zs, devices)
    came = lax.optimization_barrier((*came, src_own))[:3]
    a = (a0 + came[0]) + (came[1] + came[2])
    a = swapped(a.reshape(zs, -1, q1), "z")
    m = [m0] + [shifted(v, "x", s) for s, v in ((1, m1), (2, m2), (3, m3))]
    parts = pair_call(src_own, shifted(src_send, "core", 1))
    w_out = z_call(a, m)
    w = swapped(w_out, "z")
    parts = lax.optimization_barrier((*parts, w_out))[:4]
    parts = [parts[0]] + [shifted(parts[s], "y", s) for s in (1, 2, 3)]
    block, copies = back_call(w, parts, devices)
    shares = swapped(copies, dst_axes)
    blocks = [block] + [shifted(block, "x", s) for s in (1, 2, 3)]
    grad_src, grad_dst, grad_hour, grad_core = end_call(scales, hour_factor, blocks, shares)
    return (grad_src.reshape(src_factor.shape), grad_dst.reshape(dst_factor.shape), grad_hour, grad_core)


def solution(mesh):
    n_src, n_dst = mesh.shape["src"], mesh.shape["dst"]
    fine = Mesh(mesh.devices.reshape(n_src // X, X, n_dst // CORES, CORES), ("z", "x", "y", "core"))
    src, dst = ("z", "x"), ("y", "core")
    in_specs = (P(None, src, dst), P(src, None), P(dst, None), P(), P())
    out_specs = (P(src, None), P(dst, None), P(), P(None, src, None))

    def run(counts, src_factor, dst_factor, hour_factor, core):
        hours, total_src, total_dst = counts.shape
        scales = (1 / math.sqrt(total_dst * hours), 1 / math.sqrt(total_src * hours),
                  1 / math.sqrt(total_src * total_dst), 1 / math.sqrt(total_src * total_dst * hours))
        body = jax.shard_map(functools.partial(shards, scales), mesh=fine, in_specs=in_specs,
                             out_specs=out_specs, check_vma=False)
        return body(counts, src_factor, dst_factor, hour_factor, core)

    return run
```

```python
import functools
import math

import jax
import jax.numpy as jnp
from jax import lax
from jax.experimental import pallas as pl
from jax.experimental.pallas import tpu as pltpu
from jax.sharding import Mesh, PartitionSpec as P

X = 4
CORES = 2
GROUP = 4
SPAN = 512
F32 = jnp.float32
BF16 = jnp.bfloat16
HBM = pl.BlockSpec(memory_space=pltpu.HBM)
VMEM = pl.BlockSpec(memory_space=pltpu.VMEM)
SMEM = pl.BlockSpec(memory_space=pltpu.SMEM)


def struct(*shape, dtype=F32):
    return jax.ShapeDtypeStruct(shape, dtype)


def params(mib):
    return pltpu.CompilerParams(vmem_limit_bytes=mib << 20)


def cost(flops, size):
    return pl.CostEstimate(flops=flops, bytes_accessed=size, transcendentals=0)


def split(x):
    hi = x.astype(BF16)
    return hi, (x - hi.astype(F32)).astype(BF16)


def mm(a, b):
    return jnp.dot(a, b, preferred_element_type=F32)


def halves(x, axis):
    return jnp.concatenate(split(x), axis=axis)


def first_kernel(hour_ref, counts_hbm, src_hbm, dst_hbm, core_hbm,
                 a0, a1, a2, a3, hours_out, through_hbm,
                 counts, src, dst, core, fit_rows, fit_cols, dst_cols, dst_rows, hi_all, lo_all, dst_sum, turned,
                 through, sems):
    hours, rows, cols = counts.shape
    rank, p1, q1 = core.shape
    steps = hours // GROUP
    x = lax.axis_index("x")
    small = [pltpu.make_async_copy(a, b, sems.at[i])
             for i, (a, b) in enumerate(((core_hbm, core), (src_hbm, src), (dst_hbm, dst)))]
    parts = [pl.ds(s * GROUP, GROUP) for s in range(steps)]
    large = [pltpu.make_async_copy(counts_hbm.at[part], counts.at[part], sems.at[3 + s])
             for s, part in enumerate(parts)]
    for copy in small + large:
        copy.start()
    small[2].wait()
    dst_rows[...] = halves(dst[...], 1)
    hi, lo = split(dst[...].T)
    dst_cols[...] = jnp.concatenate([hi, hi, lo], axis=0)
    small[0].wait()
    small[1].wait()
    hi, lo = split(src[...])
    src_rows = jnp.concatenate([hi, lo, hi], axis=1)
    for k in range(hours):
        core_hour = hour_ref[k, 0] * core[0]
        for r in range(1, rank):
            core_hour = core_hour + hour_ref[k, r] * core[r]
        hours_out[k] = core_hour
        hi, lo = split(core_hour)
        fit = mm(src_rows, jnp.concatenate([hi, hi, lo], axis=0))
        hi, lo = split(fit)
        fit_rows[k * rows:(k + 1) * rows] = jnp.concatenate([hi, lo, hi], axis=1)
        fit_cols[k] = halves(fit.T, 0)
    sends = []
    for s, part in enumerate(parts):
        large[s].wait()
        block = pl.ds(s * GROUP * rows, GROUP * rows)
        for j in range(0, cols, SPAN):
            wide = pl.ds(j, SPAN)
            fitted = mm(fit_rows[block, :], dst_cols[:, wide])
            misfit = 1.0 - counts[part, :, wide].reshape(GROUP * rows, SPAN).astype(F32) / fitted
            hi, lo = split(misfit)
            hi_all[:, wide] = hi
            lo_all[:, wide] = lo
            total = None
            for k in range(GROUP):
                left = fit_cols[s * GROUP + k]
                both = mm(left, hi[k * rows:(k + 1) * rows])
                term = both[:q1] + (both[q1:] + mm(left[:q1], lo[k * rows:(k + 1) * rows]))
                total = term if total is None else total + term
            if s == 0:
                dst_sum[:, wide] = total
            else:
                dst_sum[:, wide] += total
        both = mm(hi_all[...], dst_rows[...])
        through[block, :] = both[:, :q1] + (both[:, q1:] + mm(lo_all[...], dst_rows[:, :q1]))
        sends.append(pltpu.make_async_copy(through.at[block], through_hbm.at[block], sems.at[3 + steps + s]))
        sends[-1].start()
    turned[...] = dst_sum[...].T.reshape(turned.shape)
    for s, out in enumerate((a0, a1, a2, a3)):
        out[...] = turned[lax.rem(x + s, X)]
    for copy in sends:
        copy.wait()


def first_call(hour, counts, src, dst, core):
    hours, rows, cols = counts.shape
    rank, p1, q1 = core.shape
    block = cols // X
    out = [struct(block, q1)] * X + [struct(hours, p1, q1), struct(hours * rows, q1)]
    return pl.pallas_call(
        first_kernel,
        out_shape=out,
        in_specs=[SMEM] + [HBM] * 4,
        out_specs=[VMEM] * (X + 1) + [HBM],
        scratch_shapes=[
            pltpu.VMEM(counts.shape, jnp.int32),
            pltpu.VMEM(src.shape, F32),
            pltpu.VMEM(dst.shape, F32),
            pltpu.VMEM(core.shape, F32),
            pltpu.VMEM((hours * rows, 3 * q1), BF16),
            pltpu.VMEM((hours, 2 * q1, rows), BF16),
            pltpu.VMEM((3 * q1, cols), BF16),
            pltpu.VMEM((cols, 2 * q1), BF16),
            pltpu.VMEM((GROUP * rows, cols), BF16),
            pltpu.VMEM((GROUP * rows, cols), BF16),
            pltpu.VMEM((q1, cols), F32),
            pltpu.VMEM((X, block, q1), F32),
            pltpu.VMEM((hours * rows, q1), F32),
            pltpu.SemaphoreType.DMA((3 + 2 * (hours // GROUP),)),
        ],
        compiler_params=params(60),
        cost_estimate=cost(2 * 9 * counts.size * q1, 14 << 20),
        name="misfit_terms",
    )(hour, counts, src, dst, core)


def second_kernel(through, src, core, core_hours,
                  m0, m1, m2, m3, src_own, src_send,
                  projected, rowsums, message):
    hours = core_hours.shape[0]
    rows = src.shape[0]
    rank, p1, q1 = core.shape
    zs = message.shape[1]
    x, c = lax.axis_index("x"), lax.axis_index("core")
    src_cols = halves(src[...].T, 0)
    src_sum = None
    for k in range(hours):
        th = halves(through[k * rows:(k + 1) * rows, :], 1)
        right = halves(core_hours[k].T, 1)
        both = mm(th, jnp.concatenate([right, right], axis=0))
        both = both[:, :p1] + both[:, p1:]
        src_sum = both if src_sum is None else src_sum + both
        both = mm(src_cols, th)
        both = both[:p1] + both[p1:]
        projected[k] = both[:, :q1] + both[:, q1:]
    half = rows // CORES

    @pl.when(c == 0)
    def _():
        src_own[...] = src_sum[:half]
        src_send[...] = src_sum[half:]

    @pl.when(c == 1)
    def _():
        src_own[...] = src_sum[half:]
        src_send[...] = src_sum[:half]

    for k in range(hours):
        here = projected[k]
        for r in range(rank):
            product = (here * core[r]).reshape(p1 // 8, 8, q1)
            at = k * rank + r
            rowsums[at:at + 1, :] = jnp.sum(jnp.sum(product, axis=0), axis=0, keepdims=True)
        for z in range(zs):
            for b in range(X):
                start = (z * X + b) * 4
                message[b, z, 4 * k:4 * k + 4, :] = here[start:start + 4]
    sums = jnp.sum(rowsums[...].T, axis=0, keepdims=True)
    spare = jnp.zeros((8 - sums.shape[1] // 128, 128), F32)
    tail = jnp.concatenate([sums[:, i:i + 128] for i in range(0, sums.shape[1], 128)] + [spare], axis=0)
    for s, out in enumerate((m0, m1, m2, m3)):
        out[:zs] = message[lax.rem(x + s, X)]
        out[zs, :8, :] = tail


def second_call(through, src, core, core_hours, zs):
    hours = core_hours.shape[0]
    rows = src.shape[0]
    rank, p1, q1 = core.shape
    share = hours * p1 // (zs * X)
    return pl.pallas_call(
        second_kernel,
        out_shape=[struct(zs + 1, share, q1)] * X + [struct(rows // CORES, p1)] * 2,
        in_specs=[VMEM] * 4,
        out_specs=[VMEM] * (X + 2),
        scratch_shapes=[
            pltpu.VMEM((hours, p1, q1), F32),
            pltpu.VMEM((hours * rank, q1), F32),
            pltpu.VMEM((X, zs, share, q1), F32),
        ],
        compiler_params=params(16),
        cost_estimate=cost(2 << 30, 12 << 20),
        name="src_and_projected",
    )(through, src, core, core_hours)


def sum_kernel(a0, a1, a2, a3, out):
    out[...] = (a0[...] + a1[...]) + (a2[...] + a3[...])


def sum_call(parts):
    return pl.pallas_call(
        sum_kernel, out_shape=struct(*parts[0].shape), in_specs=[VMEM] * 4, out_specs=VMEM,
        compiler_params=params(4), cost_estimate=cost(1 << 34, 1 << 20), name="x_sums",
    )(*parts)


def z_kernel(a, m0, m1, m2, m3, out):
    zs, share, _ = a.shape
    total = jnp.sum(a[...], axis=0)
    m = (m0[...] + m1[...]) + (m2[...] + m3[...])
    for z in range(zs):
        out[z, :share, :] = total
        out[z, share:2 * share, :] = m[z]
        out[z, 2 * share:, :] = m[zs, :8]


def z_call(a, m):
    zs, share, q1 = a.shape
    return pl.pallas_call(
        z_kernel, out_shape=struct(zs, 2 * share + 8, q1), in_specs=[VMEM] * 5, out_specs=VMEM,
        compiler_params=params(8), cost_estimate=cost(1 << 20, 1 << 20), name="z_terms",
    )(a, *m)


def back_kernel(w, src_own, src_came, block, copies):
    zs, rows, _ = w.shape
    share = (rows - 8) // 2
    tail = w[0, share:, :]
    block[:share, :] = w[0, :share, :]
    for z in range(1, zs):
        block[z * share:(z + 1) * share, :] = w[z, :share, :]
        tail = tail + w[z, share:, :]
    total = src_own[...] + src_came[...]
    for d in range(copies.shape[0]):
        copies[d, :share + 8, :] = tail
        copies[d, share + 8:, :] = total


def back_call(w, src_own, src_came, devices):
    zs, rows, q1 = w.shape
    share = (rows - 8) // 2
    return pl.pallas_call(
        back_kernel,
        out_shape=[struct(zs * share, q1), struct(devices, rows - share + src_own.shape[0], q1)],
        in_specs=[VMEM] * 3, out_specs=[VMEM] * 2,
        compiler_params=params(8), cost_estimate=cost(1 << 20, 1 << 20), name="z_sums",
    )(w, src_own, src_came)


def end_kernel(scales, hour_ref, b0, b1, b2, b3, d, src_out, dst_out, hour_out, core_out):
    x = lax.axis_index("x")
    src_scale, dst_scale, hour_scale, core_scale = scales
    for s, block in enumerate((b0, b1, b2, b3)):
        dst_out[lax.rem(x - s + X, X)] = block[...] * dst_scale
    hours, rank = hour_ref.shape
    share = 4 * hours
    total = jnp.sum(d[:, :share + 8, :], axis=0)
    for c in range(CORES):
        half = d[c, share + 8:, :]
        for at in range(c + CORES, d.shape[0], CORES):
            half = half + d[at, share + 8:, :]
        src_out[c] = half * src_scale
    each = 128 // rank
    for k in range(hours):
        row = share + k // each
        hour_out[k:k + 1, :] = total[row:row + 1, k % each * rank:(k % each + 1) * rank] * hour_scale
    tiles = [total[4 * k:4 * k + 4] * core_scale for k in range(hours)]
    for r in range(rank):
        out = hour_ref[0, r] * tiles[0]
        for k in range(1, hours):
            out = out + hour_ref[k, r] * tiles[k]
        core_out[r] = out


def end_call(scales, hour, blocks, d):
    block, q1 = blocks[0].shape
    hours, rank = hour.shape
    return pl.pallas_call(
        functools.partial(end_kernel, scales),
        in_specs=[SMEM] + [VMEM] * (X + 1),
        out_specs=[VMEM] * 4,
        out_shape=[struct(CORES, d.shape[1] - 4 * hours - 8, q1), struct(X, block, q1),
                   struct(hours, rank), struct(rank, 4, q1)],
        compiler_params=params(8), cost_estimate=cost(1 << 20, 1 << 20), name="outputs",
    )(hour, *blocks, d)


def shifted(x, axis, s):
    n = lax.axis_size(axis)
    return lax.ppermute(x, axis, [(i, (i + s) % n) for i in range(n)])


def swapped(x, axis):
    return lax.all_to_all(x, axis, split_axis=0, concat_axis=0, tiled=True)


def shards(scales, counts, src_factor, dst_factor, hour_factor, core):
    zs = lax.axis_size("z")
    dst_axes = ("y", "core")
    devices = lax.axis_size(dst_axes)
    q1 = dst_factor.shape[1]
    a0, a1, a2, a3, core_hours, through = first_call(hour_factor, counts, src_factor, dst_factor, core)
    came = [shifted(a, "x", s) for s, a in ((1, a1), (2, a2), (3, a3))]
    m0, m1, m2, m3, src_own, src_send = second_call(through, src_factor, core, core_hours, zs)
    src_came = shifted(src_send, "core", 1)
    m = [m0] + [shifted(v, "x", s) for s, v in ((1, m1), (2, m2), (3, m3))]
    came = lax.optimization_barrier((*came, src_own))[:3]
    a = sum_call([a0, *came])
    a = swapped(a.reshape(zs, -1, q1), "z")
    w = swapped(z_call(a, m), "z")
    block, copies = back_call(w, src_own, src_came, devices)
    shares = swapped(copies, dst_axes)
    blocks = [block] + [shifted(block, "x", s) for s in (1, 2, 3)]
    grad_src, grad_dst, grad_hour, grad_core = end_call(scales, hour_factor, blocks, shares)
    return (grad_src.reshape(src_factor.shape), grad_dst.reshape(dst_factor.shape), grad_hour, grad_core)


def solution(mesh):
    n_src, n_dst = mesh.shape["src"], mesh.shape["dst"]
    fine = Mesh(mesh.devices.reshape(n_src // X, X, n_dst // CORES, CORES), ("z", "x", "y", "core"))
    src, dst = ("z", "x"), ("y", "core")
    in_specs = (P(None, src, dst), P(src, None), P(dst, None), P(), P())
    out_specs = (P(src, None), P(dst, None), P(), P(None, src, None))

    def run(counts, src_factor, dst_factor, hour_factor, core):
        hours, total_src, total_dst = counts.shape
        scales = (1 / math.sqrt(total_dst * hours), 1 / math.sqrt(total_src * hours),
                  1 / math.sqrt(total_src * total_dst), 1 / math.sqrt(total_src * total_dst * hours))
        body = jax.shard_map(functools.partial(shards, scales), mesh=fine, in_specs=in_specs,
                             out_specs=out_specs, check_vma=False)
        return body(counts, src_factor, dst_factor, hour_factor, core)

    return run
```

```python
import functools
import math

import jax
import jax.numpy as jnp
from jax import lax
from jax.experimental import pallas as pl
from jax.experimental.pallas import tpu as pltpu
from jax.sharding import Mesh, PartitionSpec as P

X = 4
CORES = 2
GROUP = 4
SPAN = 512
F32 = jnp.float32
BF16 = jnp.bfloat16
HBM = pl.BlockSpec(memory_space=pltpu.HBM)
VMEM = pl.BlockSpec(memory_space=pltpu.VMEM)
SMEM = pl.BlockSpec(memory_space=pltpu.SMEM)


def struct(*shape, dtype=F32):
    return jax.ShapeDtypeStruct(shape, dtype)


def params(mib):
    return pltpu.CompilerParams(vmem_limit_bytes=mib << 20)


def cost(flops, size):
    return pl.CostEstimate(flops=flops, bytes_accessed=size, transcendentals=0)


def split(x):
    hi = x.astype(BF16)
    return hi, (x - hi.astype(F32)).astype(BF16)


def mm(a, b):
    return jnp.dot(a, b, preferred_element_type=F32)


def halves(x, axis):
    return jnp.concatenate(split(x), axis=axis)


def main_kernel(zs, hour_ref, counts_hbm, src_hbm, dst_hbm, core_hbm,
                m0, m1, m2, m3, src_own, src_send,
                counts, src, dst, core, fit_rows, fit_cols, dst_cols, dst_rows, hi_all, lo_all, dst_sum, turned,
                core_hours, projected, rowsums, message, sems):
    hours, rows, cols = counts.shape
    rank, p1, q1 = core.shape
    steps = hours // GROUP
    block = turned.shape[1]
    x, c = lax.axis_index("x"), lax.axis_index("core")
    outs = (m0, m1, m2, m3)
    small = [pltpu.make_async_copy(a, b, sems.at[i])
             for i, (a, b) in enumerate(((core_hbm, core), (src_hbm, src), (dst_hbm, dst)))]
    parts = [pl.ds(s * GROUP, GROUP) for s in range(steps)]
    large = [pltpu.make_async_copy(counts_hbm.at[part], counts.at[part], sems.at[3 + s])
             for s, part in enumerate(parts)]
    for copy in small + large:
        copy.start()
    small[2].wait()
    dst_rows[...] = halves(dst[...], 1)
    hi, lo = split(dst[...].T)
    dst_cols[...] = jnp.concatenate([hi, hi, lo], axis=0)
    small[0].wait()
    small[1].wait()
    hi, lo = split(src[...])
    src_rows = jnp.concatenate([hi, lo, hi], axis=1)
    for k in range(hours):
        core_hour = hour_ref[k, 0] * core[0]
        for r in range(1, rank):
            core_hour = core_hour + hour_ref[k, r] * core[r]
        core_hours[k] = core_hour
        hi, lo = split(core_hour)
        fit = mm(src_rows, jnp.concatenate([hi, hi, lo], axis=0))
        hi, lo = split(fit)
        fit_rows[k * rows:(k + 1) * rows] = jnp.concatenate([hi, lo, hi], axis=1)
        fit_cols[k] = halves(fit.T, 0)
    src_cols = halves(src[...].T, 0)
    src_sum = None
    for s, part in enumerate(parts):
        large[s].wait()
        for j in range(0, cols, SPAN):
            wide = pl.ds(j, SPAN)
            fitted = mm(fit_rows[s * GROUP * rows:(s + 1) * GROUP * rows, :], dst_cols[:, wide])
            misfit = 1.0 - counts[part, :, wide].reshape(GROUP * rows, SPAN).astype(F32) / fitted
            hi, lo = split(misfit)
            hi_all[:, wide] = hi
            lo_all[:, wide] = lo
            total = None
            for k in range(GROUP):
                left = fit_cols[s * GROUP + k]
                both = mm(left, hi[k * rows:(k + 1) * rows])
                term = both[:q1] + (both[q1:] + mm(left[:q1], lo[k * rows:(k + 1) * rows]))
                total = term if total is None else total + term
            if s == 0:
                dst_sum[:, wide] = total
            else:
                dst_sum[:, wide] += total
        both = mm(hi_all[...], dst_rows[...])
        through = both[:, :q1] + (both[:, q1:] + mm(lo_all[...], dst_rows[:, :q1]))
        for i in range(GROUP):
            k = s * GROUP + i
            th = halves(through[i * rows:(i + 1) * rows], 1)
            right = halves(core_hours[k].T, 1)
            both = mm(th, jnp.concatenate([right, right], axis=0))
            both = both[:, :p1] + both[:, p1:]
            src_sum = both if src_sum is None else src_sum + both
            both = mm(src_cols, th)
            both = both[:p1] + both[p1:]
            projected[k] = both[:, :q1] + both[:, q1:]
    turned[...] = dst_sum[...].T.reshape(turned.shape)
    places = [lax.rem(x + s, X) for s in range(X)]
    sends = [pltpu.make_async_copy(turned.at[place], out.at[pl.ds(0, block)], sems.at[3 + steps + i])
             for i, (place, out) in enumerate(zip(places, outs))]
    for copy in sends:
        copy.start()
    half = rows // CORES

    @pl.when(c == 0)
    def _():
        src_own[...] = src_sum[:half]
        src_send[...] = src_sum[half:]

    @pl.when(c == 1)
    def _():
        src_own[...] = src_sum[half:]
        src_send[...] = src_sum[:half]

    for k in range(hours):
        here = projected[k]
        for r in range(rank):
            product = (here * core[r]).reshape(p1 // 8, 8, q1)
            at = k * rank + r
            rowsums[at:at + 1, :] = jnp.sum(jnp.sum(product, axis=0), axis=0, keepdims=True)
        for z in range(zs):
            for b in range(X):
                start = (z * X + b) * 4
                row = z * 4 * hours + 4 * k
                message[b, row:row + 4, :] = here[start:start + 4]
    sums = jnp.sum(rowsums[...].T, axis=0, keepdims=True)
    spare = jnp.zeros((8 - sums.shape[1] // 128, 128), F32)
    tail = jnp.concatenate([sums[:, i:i + 128] for i in range(0, sums.shape[1], 128)] + [spare], axis=0)
    size = message.shape[1]
    for b in range(X):
        message[b, size - 8:, :] = tail
    more = [pltpu.make_async_copy(message.at[place], out.at[pl.ds(block, size)], sems.at[3 + steps + X + i])
            for i, (place, out) in enumerate(zip(places, outs))]
    for copy in more:
        copy.start()
    for copy in sends + more:
        copy.wait()


def main_call(hour, counts, src, dst, core, zs):
    hours, rows, cols = counts.shape
    rank, p1, q1 = core.shape
    block = cols // X
    size = hours * p1 // X + 8
    return pl.pallas_call(
        functools.partial(main_kernel, zs),
        out_shape=[struct(block + size, q1)] * X + [struct(rows // CORES, p1)] * 2,
        in_specs=[SMEM] + [HBM] * 4,
        out_specs=[HBM] * X + [VMEM] * 2,
        scratch_shapes=[
            pltpu.VMEM(counts.shape, jnp.int32),
            pltpu.VMEM(src.shape, F32),
            pltpu.VMEM(dst.shape, F32),
            pltpu.VMEM(core.shape, F32),
            pltpu.VMEM((hours * rows, 3 * q1), BF16),
            pltpu.VMEM((hours, 2 * q1, rows), BF16),
            pltpu.VMEM((3 * q1, cols), BF16),
            pltpu.VMEM((cols, 2 * q1), BF16),
            pltpu.VMEM((GROUP * rows, cols), BF16),
            pltpu.VMEM((GROUP * rows, cols), BF16),
            pltpu.VMEM((q1, cols), F32),
            pltpu.VMEM((X, block, q1), F32),
            pltpu.VMEM((hours, p1, q1), F32),
            pltpu.VMEM((hours, p1, q1), F32),
            pltpu.VMEM((hours * rank, q1), F32),
            pltpu.VMEM((X, size, q1), F32),
            pltpu.SemaphoreType.DMA((3 + hours // GROUP + 2 * X,)),
        ],
        compiler_params=params(60),
        cost_estimate=cost(2 * 9 * counts.size * q1, 14 << 20),
        name="all_terms",
    )(hour, counts, src, dst, core)


def small_call(kernel, name, outs, args, flops=1 << 20):
    return pl.pallas_call(
        kernel, out_shape=outs, in_specs=[VMEM] * len(args), out_specs=jax.tree.map(lambda _: VMEM, outs),
        compiler_params=params(4), cost_estimate=cost(flops, 1 << 20), name=name,
    )(*args)


def hold_kernel(a, out):
    out[...] = a[...]


def sum_kernel(*refs):
    parts = [ref[...] for ref in refs[:-1]]
    while len(parts) > 1:
        half = len(parts) // 2
        parts = [a + b for a, b in zip(parts[:half], parts[half:])]
    refs[-1][...] = parts[0]


def summed(name, *parts):
    return small_call(sum_kernel, name, struct(*parts[0].shape), parts)


def x_kernel(m0, m1, m2, m3, out):
    zs, rows, _ = out.shape
    share = (rows - 8) // 2
    block = share * zs
    m = (m0[...] + m2[...]) + (m1[...] + m3[...])
    for z in range(zs):
        out[z, :share, :] = m[z * share:(z + 1) * share]
        out[z, share:2 * share, :] = m[block + z * share:block + (z + 1) * share]
        out[z, 2 * share:, :] = m[2 * block:]


def z_kernel(w, copies, tail):
    share = copies.shape[1]
    total = jnp.sum(w[...], axis=0)
    for z in range(copies.shape[0]):
        copies[z] = total[:share]
    tail[...] = total[share:]


def end_kernel(scales, hour_ref, b0, b1, b2, b3, t0, t1, src_own, src_other,
               src_out, dst_out, hour_out, core_out):
    x, c = lax.axis_index("x"), lax.axis_index("core")
    src_scale, dst_scale, hour_scale, core_scale = scales
    for s, block in enumerate((b0, b1, b2, b3)):
        dst_out[lax.rem(x - s + X, X)] = block[...] * dst_scale
    src_out[c] = src_own[...] * src_scale
    src_out[1 - c] = src_other[...] * src_scale
    hours, rank = hour_ref.shape
    share = 4 * hours
    total = t0[...] + t1[...]
    each = 128 // rank
    for k in range(hours):
        row = share + k // each
        hour_out[k:k + 1, :] = total[row:row + 1, k % each * rank:(k % each + 1) * rank] * hour_scale
    tiles = [total[4 * k:4 * k + 4] * core_scale for k in range(hours)]
    for r in range(rank):
        out = hour_ref[0, r] * tiles[0]
        for k in range(1, hours):
            out = out + hour_ref[k, r] * tiles[k]
        core_out[r] = out


def end_call(scales, hour, blocks, tails, src_own, src_other):
    block, q1 = blocks[0].shape
    hours, rank = hour.shape
    return pl.pallas_call(
        functools.partial(end_kernel, scales),
        in_specs=[SMEM] + [VMEM] * 8,
        out_specs=[VMEM] * 4,
        out_shape=[struct(CORES, *src_own.shape), struct(X, block, q1), struct(hours, rank), struct(rank, 4, q1)],
        compiler_params=params(8), cost_estimate=cost(1 << 20, 1 << 20), name="outputs",
    )(hour, *blocks, *tails, src_own, src_other)


def shifted(x, axis, s):
    n = lax.axis_size(axis)
    return lax.ppermute(x, axis, [(i, (i + s) % n) for i in range(n)])


def swapped(x, axis):
    return lax.all_to_all(x, axis, split_axis=0, concat_axis=0, tiled=True)


def paired(x, axis, flip):
    n = lax.axis_size(axis)
    return lax.ppermute(x, axis, [(i, flip(i, n)) for i in range(n)])


def around(x, axis):
    return [x] + [shifted(x, axis, s) for s in range(1, lax.axis_size(axis))]


def shards(scales, counts, src_factor, dst_factor, hour_factor, core):
    zs = lax.axis_size("z")
    q1 = dst_factor.shape[1]
    hours = counts.shape[0]
    *m, src_own, src_send = main_call(hour_factor, counts, src_factor, dst_factor, core, zs)
    kept = small_call(hold_kernel, "kept", struct(*m[0].shape), [m[0]])
    m = [kept] + [shifted(m[s], "x", s) for s in (1, 2, 3)]
    src_half = summed("src_core_sum", src_own, shifted(src_send, "core", 1))
    src_half = summed("src_y_sum", *around(src_half, "y"))
    src_other = shifted(src_half, "core", 1)
    m = lax.optimization_barrier((*m, src_half))[:X]
    share = dst_factor.shape[0] // X // zs
    w = small_call(x_kernel, "x_sums", struct(zs, 2 * share + 8, q1), m)
    copies, tail = small_call(z_kernel, "z_sums", [struct(zs, share, q1), struct(share + 8, q1)], [swapped(w, "z")])
    tail = summed("core_sum", tail, shifted(tail, "core", 1))
    tail = summed("near_sum", tail, paired(tail, "y", lambda i, n: i ^ 1))
    block = swapped(copies, "z").reshape(zs * share, q1)
    block = lax.optimization_barrier((block, tail))[0]
    tails = [tail, paired(tail, "y", lambda i, n: n - 1 - i)]
    blocks = around(block, "x")
    grad_src, grad_dst, grad_hour, grad_core = end_call(scales, hour_factor, blocks, tails, src_half, src_other)
    return (grad_src.reshape(src_factor.shape), grad_dst.reshape(dst_factor.shape), grad_hour, grad_core)


def solution(mesh):
    n_src, n_dst = mesh.shape["src"], mesh.shape["dst"]
    fine = Mesh(mesh.devices.reshape(n_src // X, X, n_dst // CORES, CORES), ("z", "x", "y", "core"))
    src, dst = ("z", "x"), ("y", "core")
    in_specs = (P(None, src, dst), P(src, None), P(dst, None), P(), P())
    out_specs = (P(src, None), P(dst, None), P(), P(None, src, None))

    def run(counts, src_factor, dst_factor, hour_factor, core):
        hours, total_src, total_dst = counts.shape
        scales = (1 / math.sqrt(total_dst * hours), 1 / math.sqrt(total_src * hours),
                  1 / math.sqrt(total_src * total_dst), 1 / math.sqrt(total_src * total_dst * hours))
        body = jax.shard_map(functools.partial(shards, scales), mesh=fine, in_specs=in_specs,
                             out_specs=out_specs, check_vma=False)
        return body(counts, src_factor, dst_factor, hour_factor, core)

    return run
```

```python
import functools
import math

import jax
import jax.numpy as jnp
from jax import lax
from jax.experimental import pallas as pl
from jax.experimental.pallas import tpu as pltpu
from jax.sharding import Mesh, PartitionSpec as P

X = 4
CORES = 2
GROUP = 4
SPAN = 512
F32 = jnp.float32
BF16 = jnp.bfloat16
HBM = pl.BlockSpec(memory_space=pltpu.HBM)
VMEM = pl.BlockSpec(memory_space=pltpu.VMEM)
SMEM = pl.BlockSpec(memory_space=pltpu.SMEM)


def struct(*shape, dtype=F32):
    return jax.ShapeDtypeStruct(shape, dtype)


def params(mib):
    return pltpu.CompilerParams(vmem_limit_bytes=mib << 20)


def cost(flops, size):
    return pl.CostEstimate(flops=flops, bytes_accessed=size, transcendentals=0)


def split(x):
    hi = x.astype(BF16)
    return hi, (x - hi.astype(F32)).astype(BF16)


def mm(a, b):
    return jnp.dot(a, b, preferred_element_type=F32)


def halves(x, axis):
    return jnp.concatenate(split(x), axis=axis)


def main_kernel(hour_ref, counts_hbm, src_hbm, dst_hbm, core_hbm,
                a0, a1, a2, a3, own, send,
                counts, src, dst, core, fit_rows, fit_cols, dst_cols, dst_rows, hi_all, lo_all, dst_sum, turned,
                core_hours, projected, src_all, sems):
    hours, rows, cols = counts.shape
    rank, p1, q1 = core.shape
    steps = hours // GROUP
    x, c = lax.axis_index("x"), lax.axis_index("core")
    small = [pltpu.make_async_copy(a, b, sems.at[i])
             for i, (a, b) in enumerate(((core_hbm, core), (src_hbm, src), (dst_hbm, dst)))]
    parts = [pl.ds(s * GROUP, GROUP) for s in range(steps)]
    large = [pltpu.make_async_copy(counts_hbm.at[part], counts.at[part], sems.at[3 + s])
             for s, part in enumerate(parts)]
    for copy in small + large:
        copy.start()
    small[2].wait()
    dst_rows[...] = halves(dst[...], 1)
    hi, lo = split(dst[...].T)
    dst_cols[...] = jnp.concatenate([hi, hi, lo], axis=0)
    small[0].wait()
    small[1].wait()
    hi, lo = split(src[...])
    src_rows = jnp.concatenate([hi, lo, hi], axis=1)
    for k in range(hours):
        core_hour = hour_ref[k, 0] * core[0]
        for r in range(1, rank):
            core_hour = core_hour + hour_ref[k, r] * core[r]
        core_hours[k] = core_hour
        hi, lo = split(core_hour)
        fit = mm(src_rows, jnp.concatenate([hi, hi, lo], axis=0))
        hi, lo = split(fit)
        fit_rows[k * rows:(k + 1) * rows] = jnp.concatenate([hi, lo, hi], axis=1)
        fit_cols[k] = halves(fit.T, 0)
    src_cols = halves(src[...].T, 0)
    src_sum = None
    for s, part in enumerate(parts):
        large[s].wait()
        for j in range(0, cols, SPAN):
            wide = pl.ds(j, SPAN)
            fitted = mm(fit_rows[s * GROUP * rows:(s + 1) * GROUP * rows, :], dst_cols[:, wide])
            misfit = 1.0 - counts[part, :, wide].reshape(GROUP * rows, SPAN).astype(F32) / fitted
            hi, lo = split(misfit)
            hi_all[:, wide] = hi
            lo_all[:, wide] = lo
            total = None
            for k in range(GROUP):
                left = fit_cols[s * GROUP + k]
                both = mm(left, hi[k * rows:(k + 1) * rows])
                term = both[:q1] + (both[q1:] + mm(left[:q1], lo[k * rows:(k + 1) * rows]))
                total = term if total is None else total + term
            if s == 0:
                dst_sum[:, wide] = total
            else:
                dst_sum[:, wide] += total
        both = mm(hi_all[...], dst_rows[...])
        through = both[:, :q1] + (both[:, q1:] + mm(lo_all[...], dst_rows[:, :q1]))
        for i in range(GROUP):
            k = s * GROUP + i
            th = halves(through[i * rows:(i + 1) * rows], 1)
            right = halves(core_hours[k].T, 1)
            both = mm(th, jnp.concatenate([right, right], axis=0))
            both = both[:, :p1] + both[:, p1:]
            src_sum = both if src_sum is None else src_sum + both
            both = mm(src_cols, th)
            both = both[:p1] + both[p1:]
            projected[k] = both[:, :q1] + both[:, q1:]
    turned[...] = dst_sum[...].T.reshape(turned.shape)
    src_all[...] = src_sum.reshape(src_all.shape)
    first = 3 + steps
    moves = [(turned.at[lax.rem(x + s, X)], out) for s, out in enumerate((a0, a1, a2, a3))]
    half = hours // CORES
    for mine, out in ((c, own), (1 - c, send)):
        moves.append((projected.at[pl.ds(mine * half, half)], out.at[pl.ds(0, half)]))
        moves.append((src_all.at[pl.ds(mine, 1)], out.at[pl.ds(half, 1)]))
    copies = [pltpu.make_async_copy(a, b, sems.at[first + i]) for i, (a, b) in enumerate(moves)]
    for copy in copies:
        copy.start()
    for copy in copies:
        copy.wait()


def main_call(hour, counts, src, dst, core):
    hours, rows, cols = counts.shape
    rank, p1, q1 = core.shape
    block = cols // X
    half = hours // CORES + 1
    return pl.pallas_call(
        main_kernel,
        out_shape=[struct(block, q1)] * X + [struct(half, p1, q1)] * 2,
        in_specs=[SMEM] + [HBM] * 4,
        out_specs=[HBM] * (X + 2),
        scratch_shapes=[
            pltpu.VMEM(counts.shape, jnp.int32),
            pltpu.VMEM(src.shape, F32),
            pltpu.VMEM(dst.shape, F32),
            pltpu.VMEM(core.shape, F32),
            pltpu.VMEM((hours * rows, 3 * q1), BF16),
            pltpu.VMEM((hours, 2 * q1, rows), BF16),
            pltpu.VMEM((3 * q1, cols), BF16),
            pltpu.VMEM((cols, 2 * q1), BF16),
            pltpu.VMEM((GROUP * rows, cols), BF16),
            pltpu.VMEM((GROUP * rows, cols), BF16),
            pltpu.VMEM((q1, cols), F32),
            pltpu.VMEM((X, block, q1), F32),
            pltpu.VMEM((hours, p1, q1), F32),
            pltpu.VMEM((hours, p1, q1), F32),
            pltpu.VMEM((CORES, rows // CORES, p1), F32),
            pltpu.SemaphoreType.DMA((3 + hours // GROUP + X + 4,)),
        ],
        compiler_params=params(60),
        cost_estimate=cost(2 * 9 * counts.size * q1, 14 << 20),
        name="all_terms",
    )(hour, counts, src, dst, core)


def share_kernel(zs, own, came, core, m0, m1, m2, m3, src_half, rowsums, message):
    half = own.shape[0] - 1
    rank, p1, q1 = core.shape
    x = lax.axis_index("x")
    src_half[...] = own[half] + came[half]
    for k in range(half):
        here = own[k] + came[k]
        for r in range(rank):
            product = (here * core[r]).reshape(p1 // 8, 8, q1)
            at = k * rank + r
            rowsums[at:at + 1, :] = jnp.sum(jnp.sum(product, axis=0), axis=0, keepdims=True)
        for z in range(zs):
            for b in range(X):
                start = (z * X + b) * 4
                row = (z * half + k) * 4
                message[b, row:row + 4, :] = here[start:start + 4]
    sums = jnp.sum(rowsums[...].T, axis=0, keepdims=True)
    tail = jnp.concatenate([sums, jnp.zeros((7, q1), F32)], axis=0)
    size = message.shape[1]
    for s, out in enumerate((m0, m1, m2, m3)):
        out[:size, :] = message[lax.rem(x + s, X)]
        out[size:, :] = tail


def share_call(own, came, core, zs):
    half = own.shape[0] - 1
    rank, p1, q1 = core.shape
    size = half * p1 // X
    return pl.pallas_call(
        functools.partial(share_kernel, zs),
        out_shape=[struct(size + 8, q1)] * X + [struct(p1, q1)],
        in_specs=[VMEM] * 3,
        out_specs=[VMEM] * (X + 1),
        scratch_shapes=[pltpu.VMEM((half * rank, q1), F32), pltpu.VMEM((X, size, q1), F32)],
        compiler_params=params(8),
        cost_estimate=cost(1 << 34, 4 << 20),
        name="hour_terms",
    )(own, came, core)


def small_call(kernel, name, outs, args, flops=1 << 20):
    return pl.pallas_call(
        kernel, out_shape=outs, in_specs=[VMEM] * len(args), out_specs=jax.tree.map(lambda _: VMEM, outs),
        compiler_params=params(4), cost_estimate=cost(flops, 1 << 20), name=name,
    )(*args)


def sum_kernel(*refs):
    parts = [ref[...] for ref in refs[:-1]]
    while len(parts) > 1:
        half = len(parts) // 2
        parts = [a + b for a, b in zip(parts[:half], parts[half:])]
    refs[-1][...] = parts[0]


def summed(name, *parts):
    return small_call(sum_kernel, name, struct(*parts[0].shape), parts)


def x_kernel(a0, a1, a2, a3, m0, m1, m2, m3, out):
    zs, rows, _ = out.shape
    share = a0.shape[0] // zs
    each = rows - share - 8
    a = (a0[...] + a2[...]) + (a1[...] + a3[...])
    m = (m0[...] + m2[...]) + (m1[...] + m3[...])
    for z in range(zs):
        out[z, :share, :] = a[z * share:(z + 1) * share]
        out[z, share:share + each, :] = m[z * each:(z + 1) * each]
        out[z, share + each:, :] = m[zs * each:]


def z_kernel(w, copies, tail):
    share = copies.shape[1]
    total = jnp.sum(w[...], axis=0)
    for z in range(copies.shape[0]):
        copies[z] = total[:share]
    tail[...] = total[share:]


def end_kernel(scales, hour_ref, b0, b1, b2, b3, own, other, src_own, src_other,
               src_out, dst_out, hour_out, core_out, both):
    x, c = lax.axis_index("x"), lax.axis_index("core")
    src_scale, dst_scale, hour_scale, core_scale = scales
    for s, block in enumerate((b0, b1, b2, b3)):
        dst_out[lax.rem(x - s + X, X)] = block[...] * dst_scale
    src_out[c] = src_own[...] * src_scale
    src_out[1 - c] = src_other[...] * src_scale
    both[c] = own[...]
    both[1 - c] = other[...]
    hours, rank = hour_ref.shape
    half = hours // CORES
    tiles = []
    for k in range(hours):
        at, i = k // half, k % half
        hour_out[k:k + 1, :] = both[at, 4 * half:4 * half + 1, i * rank:(i + 1) * rank] * hour_scale
        tiles.append(both[at, 4 * i:4 * i + 4, :] * core_scale)
    for r in range(rank):
        out = hour_ref[0, r] * tiles[0]
        for k in range(1, hours):
            out = out + hour_ref[k, r] * tiles[k]
        core_out[r] = out


def end_call(scales, hour, blocks, own, other, src_own, src_other):
    block, q1 = blocks[0].shape
    hours, rank = hour.shape
    return pl.pallas_call(
        functools.partial(end_kernel, scales),
        in_specs=[SMEM] + [VMEM] * 8,
        out_specs=[VMEM] * 4,
        out_shape=[struct(CORES, *src_own.shape), struct(X, block, q1), struct(hours, rank), struct(rank, 4, q1)],
        scratch_shapes=[pltpu.VMEM((CORES, *own.shape), F32)],
        compiler_params=params(8), cost_estimate=cost(1 << 20, 1 << 20), name="outputs",
    )(hour, *blocks, own, other, src_own, src_other)


def shifted(x, axis, s):
    n = lax.axis_size(axis)
    return lax.ppermute(x, axis, [(i, (i + s) % n) for i in range(n)])


def swapped(x, axis):
    return lax.all_to_all(x, axis, split_axis=0, concat_axis=0, tiled=True)


def paired(x, axis, flip):
    n = lax.axis_size(axis)
    return lax.ppermute(x, axis, [(i, flip(i, n)) for i in range(n)])


def around(x, axis):
    return [x] + [shifted(x, axis, s) for s in range(1, lax.axis_size(axis))]


def shards(scales, counts, src_factor, dst_factor, hour_factor, core):
    zs = lax.axis_size("z")
    q1 = dst_factor.shape[1]
    a0, a1, a2, a3, own, send = main_call(hour_factor, counts, src_factor, dst_factor, core)
    a = [a0] + [shifted(v, "x", s) for s, v in ((1, a1), (2, a2), (3, a3))]
    m0, m1, m2, m3, src_half = share_call(own, shifted(send, "core", 1), core, zs)
    m = [m0] + [shifted(v, "x", s) for s, v in ((1, m1), (2, m2), (3, m3))]
    share = a0.shape[0] // zs
    each = (m0.shape[0] - 8) // zs
    w = small_call(x_kernel, "x_sums", struct(zs, share + each + 8, q1), [*a, *m])
    src_half = summed("src_y_sum", *around(src_half, "y"))
    src_other = shifted(src_half, "core", 1)
    w = lax.optimization_barrier((swapped(w, "z"), src_half))[0]
    copies, tail = small_call(z_kernel, "z_sums", [struct(zs, share, q1), struct(each + 8, q1)], [w])
    tail = summed("near_sum", tail, paired(tail, "y", lambda i, n: i ^ 1))
    block = swapped(copies, "z").reshape(zs * share, q1)
    block = lax.optimization_barrier((block, tail))[0]
    tail = summed("far_sum", tail, paired(tail, "y", lambda i, n: n - 1 - i))
    other = shifted(tail, "core", 1)
    blocks = around(block, "x")
    grad_src, grad_dst, grad_hour, grad_core = end_call(
        scales, hour_factor, blocks, tail, other, src_half, src_other)
    return (grad_src.reshape(src_factor.shape), grad_dst.reshape(dst_factor.shape), grad_hour, grad_core)


def solution(mesh):
    n_src, n_dst = mesh.shape["src"], mesh.shape["dst"]
    fine = Mesh(mesh.devices.reshape(n_src // X, X, n_dst // CORES, CORES), ("z", "x", "y", "core"))
    src, dst = ("z", "x"), ("y", "core")
    in_specs = (P(None, src, dst), P(src, None), P(dst, None), P(), P())
    out_specs = (P(src, None), P(dst, None), P(), P(None, src, None))

    def run(counts, src_factor, dst_factor, hour_factor, core):
        hours, total_src, total_dst = counts.shape
        scales = (1 / math.sqrt(total_dst * hours), 1 / math.sqrt(total_src * hours),
                  1 / math.sqrt(total_src * total_dst), 1 / math.sqrt(total_src * total_dst * hours))
        body = jax.shard_map(functools.partial(shards, scales), mesh=fine, in_specs=in_specs,
                             out_specs=out_specs, check_vma=False)
        return body(counts, src_factor, dst_factor, hour_factor, core)

    return run
```

```python
import functools
import math

import jax
import jax.numpy as jnp
from jax import lax
from jax.experimental import pallas as pl
from jax.experimental.pallas import tpu as pltpu
from jax.sharding import Mesh, PartitionSpec as P

X = 4
CORES = 2
GROUP = 4
SPAN = 512
F32 = jnp.float32
BF16 = jnp.bfloat16
HBM = pl.BlockSpec(memory_space=pltpu.HBM)
VMEM = pl.BlockSpec(memory_space=pltpu.VMEM)
SMEM = pl.BlockSpec(memory_space=pltpu.SMEM)


def struct(*shape, dtype=F32):
    return jax.ShapeDtypeStruct(shape, dtype)


def params(mib):
    return pltpu.CompilerParams(vmem_limit_bytes=mib << 20)


def cost(flops, size):
    return pl.CostEstimate(flops=flops, bytes_accessed=size, transcendentals=0)


def split(x):
    hi = x.astype(BF16)
    return hi, (x - hi.astype(F32)).astype(BF16)


def mm(a, b):
    return jnp.dot(a, b, preferred_element_type=F32)


def halves(x, axis):
    return jnp.concatenate(split(x), axis=axis)


def main_kernel(hour_ref, counts_hbm, src_hbm, dst_hbm, core_hbm,
                a0, a1, a2, a3, own, send,
                counts, src, dst, core, fit_rows, fit_cols, dst_cols, dst_rows, hi_all, lo_all, dst_sum, turned,
                core_hours, projected, src_all, sems):
    hours, rows, cols = counts.shape
    rank, p1, q1 = core.shape
    steps = hours // GROUP
    x, c = lax.axis_index("x"), lax.axis_index("core")
    small = [pltpu.make_async_copy(a, b, sems.at[i])
             for i, (a, b) in enumerate(((core_hbm, core), (src_hbm, src), (dst_hbm, dst)))]
    parts = [pl.ds(s * GROUP, GROUP) for s in range(steps)]
    large = [pltpu.make_async_copy(counts_hbm.at[part], counts.at[part], sems.at[3 + s])
             for s, part in enumerate(parts)]
    for copy in small[::-1] + large:
        copy.start()
    small[2].wait()
    dst_rows[...] = halves(dst[...], 1)
    hi, lo = split(dst[...].T)
    dst_cols[...] = jnp.concatenate([hi, hi, lo], axis=0)
    small[0].wait()
    small[1].wait()
    hi, lo = split(src[...])
    src_rows = jnp.concatenate([hi, lo, hi], axis=1)
    for k in range(hours):
        core_hour = hour_ref[k, 0] * core[0]
        for r in range(1, rank):
            core_hour = core_hour + hour_ref[k, r] * core[r]
        core_hours[k] = core_hour
        hi, lo = split(core_hour)
        fit = mm(src_rows, jnp.concatenate([hi, hi, lo], axis=0))
        hi, lo = split(fit)
        fit_rows[k * rows:(k + 1) * rows] = jnp.concatenate([hi, lo, hi], axis=1)
        fit_cols[k] = halves(fit.T, 0)
    src_cols = halves(src[...].T, 0)
    src_sum = None
    for s, part in enumerate(parts):
        large[s].wait()
        for j in range(0, cols, SPAN):
            wide = pl.ds(j, SPAN)
            fitted = mm(fit_rows[s * GROUP * rows:(s + 1) * GROUP * rows, :], dst_cols[:, wide])
            misfit = 1.0 - counts[part, :, wide].reshape(GROUP * rows, SPAN).astype(F32) / fitted
            hi, lo = split(misfit)
            hi_all[:, wide] = hi
            lo_all[:, wide] = lo
            total = None
            for k in range(GROUP):
                left = fit_cols[s * GROUP + k]
                both = mm(left, hi[k * rows:(k + 1) * rows])
                term = both[:q1] + (both[q1:] + mm(left[:q1], lo[k * rows:(k + 1) * rows]))
                total = term if total is None else total + term
            if s == 0:
                dst_sum[:, wide] = total
            else:
                dst_sum[:, wide] += total
        both = mm(hi_all[...], dst_rows[...])
        through = both[:, :q1] + (both[:, q1:] + mm(lo_all[...], dst_rows[:, :q1]))
        for i in range(GROUP):
            k = s * GROUP + i
            th = halves(through[i * rows:(i + 1) * rows], 1)
            right = halves(core_hours[k].T, 1)
            both = mm(th, jnp.concatenate([right, right], axis=0))
            both = both[:, :p1] + both[:, p1:]
            src_sum = both if src_sum is None else src_sum + both
            both = mm(src_cols, th)
            both = both[:p1] + both[p1:]
            projected[k] = both[:, :q1] + both[:, q1:]
    turned[...] = dst_sum[...].T.reshape(turned.shape)
    src_all[...] = src_sum.reshape(src_all.shape)
    first = 3 + steps
    moves = [(turned.at[lax.rem(x + s, X)], out) for s, out in enumerate((a0, a1, a2, a3))]
    half = hours // CORES
    for mine, out in ((c, own), (1 - c, send)):
        moves.append((projected.at[pl.ds(mine * half, half)], out.at[pl.ds(0, half)]))
        moves.append((src_all.at[pl.ds(mine, 1)], out.at[pl.ds(half, 1)]))
    copies = [pltpu.make_async_copy(a, b, sems.at[first + i]) for i, (a, b) in enumerate(moves)]
    for copy in copies:
        copy.start()
    for copy in copies:
        copy.wait()


def main_call(hour, counts, src, dst, core):
    hours, rows, cols = counts.shape
    rank, p1, q1 = core.shape
    block = cols // X
    half = hours // CORES + 1
    return pl.pallas_call(
        main_kernel,
        out_shape=[struct(block, q1)] * X + [struct(half, p1, q1)] * 2,
        in_specs=[SMEM] + [HBM] * 4,
        out_specs=[HBM] * (X + 2),
        scratch_shapes=[
            pltpu.VMEM(counts.shape, jnp.int32),
            pltpu.VMEM(src.shape, F32),
            pltpu.VMEM(dst.shape, F32),
            pltpu.VMEM(core.shape, F32),
            pltpu.VMEM((hours * rows, 3 * q1), BF16),
            pltpu.VMEM((hours, 2 * q1, rows), BF16),
            pltpu.VMEM((3 * q1, cols), BF16),
            pltpu.VMEM((cols, 2 * q1), BF16),
            pltpu.VMEM((GROUP * rows, cols), BF16),
            pltpu.VMEM((GROUP * rows, cols), BF16),
            pltpu.VMEM((q1, cols), F32),
            pltpu.VMEM((X, block, q1), F32),
            pltpu.VMEM((hours, p1, q1), F32),
            pltpu.VMEM((hours, p1, q1), F32),
            pltpu.VMEM((CORES, rows // CORES, p1), F32),
            pltpu.SemaphoreType.DMA((3 + hours // GROUP + X + 4,)),
        ],
        compiler_params=params(60),
        cost_estimate=cost(2 * 9 * counts.size * q1, 14 << 20),
        name="all_terms",
    )(hour, counts, src, dst, core)


def share_kernel(zs, own, came, core, m0, m1, m2, m3, src_half, rowsums, message):
    half = own.shape[0] - 1
    rank, p1, q1 = core.shape
    x = lax.axis_index("x")
    src_half[...] = own[half] + came[half]
    for k in range(half):
        here = own[k] + came[k]
        for r in range(rank):
            product = (here * core[r]).reshape(p1 // 8, 8, q1)
            at = k * rank + r
            rowsums[at:at + 1, :] = jnp.sum(jnp.sum(product, axis=0), axis=0, keepdims=True)
        for z in range(zs):
            for b in range(X):
                start = (z * X + b) * 4
                row = (z * half + k) * 4
                message[b, row:row + 4, :] = here[start:start + 4]
    sums = jnp.sum(rowsums[...].T, axis=0, keepdims=True)
    tail = jnp.concatenate([sums, jnp.zeros((7, q1), F32)], axis=0)
    size = message.shape[1]
    for s, out in enumerate((m0, m1, m2, m3)):
        out[:size, :] = message[lax.rem(x + s, X)]
        out[size:, :] = tail


def share_call(own, came, core, zs):
    half = own.shape[0] - 1
    rank, p1, q1 = core.shape
    size = half * p1 // X
    return pl.pallas_call(
        functools.partial(share_kernel, zs),
        out_shape=[struct(size + 8, q1)] * X + [struct(p1, q1)],
        in_specs=[VMEM] * 3,
        out_specs=[VMEM] * (X + 1),
        scratch_shapes=[pltpu.VMEM((half * rank, q1), F32), pltpu.VMEM((X, size, q1), F32)],
        compiler_params=params(8),
        cost_estimate=cost(1 << 34, 4 << 20),
        name="hour_terms",
    )(own, came, core)


def small_call(kernel, name, outs, args, flops=1 << 20):
    return pl.pallas_call(
        kernel, out_shape=outs, in_specs=[VMEM] * len(args), out_specs=jax.tree.map(lambda _: VMEM, outs),
        compiler_params=params(4), cost_estimate=cost(flops, 1 << 20), name=name,
    )(*args)


def sum_kernel(*refs):
    parts = [ref[...] for ref in refs[:-1]]
    while len(parts) > 1:
        half = len(parts) // 2
        parts = [a + b for a, b in zip(parts[:half], parts[half:])]
    refs[-1][...] = parts[0]


def summed(name, *parts):
    return small_call(sum_kernel, name, struct(*parts[0].shape), parts)


def x_kernel(a0, a1, a2, a3, m0, m1, m2, m3, out):
    zs, rows, _ = out.shape
    share = a0.shape[0] // zs
    each = rows - share - 8
    a = (a0[...] + a2[...]) + (a1[...] + a3[...])
    m = (m0[...] + m2[...]) + (m1[...] + m3[...])
    for z in range(zs):
        out[z, :share, :] = a[z * share:(z + 1) * share]
        out[z, share:share + each, :] = m[z * each:(z + 1) * each]
        out[z, share + each:, :] = m[zs * each:]


def tail_kernel(share, w, tail):
    tail[...] = jnp.sum(w[:, share:, :], axis=0)


def z_kernel(w, copies):
    share = copies.shape[1]
    total = jnp.sum(w[:, :share, :], axis=0)
    for z in range(copies.shape[0]):
        copies[z] = total


def end_kernel(scales, hour_ref, b0, b1, b2, b3, own, other, src_own, src_other,
               src_out, dst_out, hour_out, core_out, both):
    x, c = lax.axis_index("x"), lax.axis_index("core")
    src_scale, dst_scale, hour_scale, core_scale = scales
    for s, block in enumerate((b0, b1, b2, b3)):
        dst_out[lax.rem(x - s + X, X)] = block[...] * dst_scale
    src_out[c] = src_own[...] * src_scale
    src_out[1 - c] = src_other[...] * src_scale
    both[c] = own[...]
    both[1 - c] = other[...]
    hours, rank = hour_ref.shape
    half = hours // CORES
    tiles = []
    for k in range(hours):
        at, i = k // half, k % half
        hour_out[k:k + 1, :] = both[at, 4 * half:4 * half + 1, i * rank:(i + 1) * rank] * hour_scale
        tiles.append(both[at, 4 * i:4 * i + 4, :] * core_scale)
    for r in range(rank):
        out = hour_ref[0, r] * tiles[0]
        for k in range(1, hours):
            out = out + hour_ref[k, r] * tiles[k]
        core_out[r] = out


def end_call(scales, hour, blocks, own, other, src_own, src_other):
    block, q1 = blocks[0].shape
    hours, rank = hour.shape
    return pl.pallas_call(
        functools.partial(end_kernel, scales),
        in_specs=[SMEM] + [VMEM] * 8,
        out_specs=[VMEM] * 4,
        out_shape=[struct(CORES, *src_own.shape), struct(X, block, q1), struct(hours, rank), struct(rank, 4, q1)],
        scratch_shapes=[pltpu.VMEM((CORES, *own.shape), F32)],
        compiler_params=params(8), cost_estimate=cost(1 << 20, 1 << 20), name="outputs",
    )(hour, *blocks, own, other, src_own, src_other)


def shifted(x, axis, s):
    n = lax.axis_size(axis)
    return lax.ppermute(x, axis, [(i, (i + s) % n) for i in range(n)])


def swapped(x, axis):
    return lax.all_to_all(x, axis, split_axis=0, concat_axis=0, tiled=True)


def paired(x, axis, flip):
    n = lax.axis_size(axis)
    return lax.ppermute(x, axis, [(i, flip(i, n)) for i in range(n)])


def near(i, n):
    return i ^ 1


def far(i, n):
    return n - 1 - i


def around(x, axis):
    return [x] + [shifted(x, axis, s) for s in range(1, lax.axis_size(axis))]


def shards(scales, counts, src_factor, dst_factor, hour_factor, core):
    zs = lax.axis_size("z")
    q1 = dst_factor.shape[1]
    a0, a1, a2, a3, own, send = main_call(hour_factor, counts, src_factor, dst_factor, core)
    a = [a0] + [shifted(v, "x", s) for s, v in ((1, a1), (2, a2), (3, a3))]
    m0, m1, m2, m3, src_half = share_call(own, shifted(send, "core", 1), core, zs)
    m = [m0] + [shifted(v, "x", s) for s, v in ((1, m1), (2, m2), (3, m3))]
    share = a0.shape[0] // zs
    each = (m0.shape[0] - 8) // zs
    src_half = summed("src_near_sum", src_half, paired(src_half, "y", near))
    w = small_call(x_kernel, "x_sums", struct(zs, share + each + 8, q1), [*a, *m])
    w = swapped(w, "z")
    src_half = summed("src_far_sum", src_half, paired(src_half, "y", far))
    w, src_half = lax.optimization_barrier((w, src_half))
    src_other = shifted(src_half, "core", 1)
    tail = small_call(functools.partial(tail_kernel, share), "tail_sums", struct(each + 8, q1), [w])
    came = paired(tail, "y", near)
    copies = small_call(z_kernel, "z_sums", struct(zs, share, q1), [w], 1 << 34)
    block = swapped(copies, "z").reshape(zs * share, q1)
    tail = summed("near_sum", tail, came)
    tail = summed("far_sum", tail, paired(tail, "y", far))
    block, tail = lax.optimization_barrier((block, tail))
    other = shifted(tail, "core", 1)
    blocks = around(block, "x")
    grad_src, grad_dst, grad_hour, grad_core = end_call(
        scales, hour_factor, blocks, tail, other, src_half, src_other)
    return (grad_src.reshape(src_factor.shape), grad_dst.reshape(dst_factor.shape), grad_hour, grad_core)


def solution(mesh):
    n_src, n_dst = mesh.shape["src"], mesh.shape["dst"]
    fine = Mesh(mesh.devices.reshape(n_src // X, X, n_dst // CORES, CORES), ("z", "x", "y", "core"))
    src, dst = ("z", "x"), ("y", "core")
    in_specs = (P(None, src, dst), P(src, None), P(dst, None), P(), P())
    out_specs = (P(src, None), P(dst, None), P(), P(None, src, None))

    def run(counts, src_factor, dst_factor, hour_factor, core):
        hours, total_src, total_dst = counts.shape
        scales = (1 / math.sqrt(total_dst * hours), 1 / math.sqrt(total_src * hours),
                  1 / math.sqrt(total_src * total_dst), 1 / math.sqrt(total_src * total_dst * hours))
        body = jax.shard_map(functools.partial(shards, scales), mesh=fine, in_specs=in_specs,
                             out_specs=out_specs, check_vma=False)
        return body(counts, src_factor, dst_factor, hour_factor, core)

    return run
```

```python
import functools
import math

import jax
import jax.numpy as jnp
from jax import lax
from jax.experimental import pallas as pl
from jax.experimental.pallas import tpu as pltpu
from jax.sharding import Mesh, PartitionSpec as P

X = 4
CORES = 2
GROUP = 4
SPAN = 512
F32 = jnp.float32
BF16 = jnp.bfloat16
HBM = pl.BlockSpec(memory_space=pltpu.HBM)
VMEM = pl.BlockSpec(memory_space=pltpu.VMEM)
SMEM = pl.BlockSpec(memory_space=pltpu.SMEM)


def struct(*shape, dtype=F32):
    return jax.ShapeDtypeStruct(shape, dtype)


def params(mib):
    return pltpu.CompilerParams(vmem_limit_bytes=mib << 20)


def cost(flops, size):
    return pl.CostEstimate(flops=flops, bytes_accessed=size, transcendentals=0)


def split(x):
    hi = x.astype(BF16)
    return hi, (x - hi.astype(F32)).astype(BF16)


def mm(a, b):
    return jnp.dot(a, b, preferred_element_type=F32)


def halves(x, axis):
    return jnp.concatenate(split(x), axis=axis)


def main_kernel(hour_ref, counts_hbm, src_hbm, dst_hbm, core_hbm,
                a0, a1, a2, a3, own, send,
                counts, src, dst, core, fit_rows, fit_cols, dst_cols, dst_rows, hi_all, lo_all, dst_sum, turned,
                core_hours, projected, src_all, sems):
    hours, rows, cols = counts.shape
    rank, p1, q1 = core.shape
    steps = hours // GROUP
    x, c = lax.axis_index("x"), lax.axis_index("core")
    small = [pltpu.make_async_copy(a, b, sems.at[i])
             for i, (a, b) in enumerate(((core_hbm, core), (src_hbm, src), (dst_hbm, dst)))]
    parts = [pl.ds(s * GROUP, GROUP) for s in range(steps)]
    large = [pltpu.make_async_copy(counts_hbm.at[part], counts.at[part], sems.at[3 + s])
             for s, part in enumerate(parts)]
    for copy in small[::-1] + large:
        copy.start()
    small[2].wait()
    dst_rows[...] = halves(dst[...], 1)
    hi, lo = split(dst[...].T)
    dst_cols[...] = jnp.concatenate([hi, hi, lo], axis=0)
    small[0].wait()
    small[1].wait()
    hi, lo = split(src[...])
    src_rows = jnp.concatenate([hi, lo, hi], axis=1)
    for k in range(hours):
        core_hour = hour_ref[k, 0] * core[0]
        for r in range(1, rank):
            core_hour = core_hour + hour_ref[k, r] * core[r]
        core_hours[k] = core_hour
        hi, lo = split(core_hour)
        fit = mm(src_rows, jnp.concatenate([hi, hi, lo], axis=0))
        hi, lo = split(fit)
        fit_rows[k * rows:(k + 1) * rows] = jnp.concatenate([hi, lo, hi], axis=1)
        fit_cols[k] = halves(fit.T, 0)
    src_cols = halves(src[...].T, 0)
    src_sum = None
    for s, part in enumerate(parts):
        large[s].wait()
        for j in range(0, cols, SPAN):
            wide = pl.ds(j, SPAN)
            fitted = mm(fit_rows[s * GROUP * rows:(s + 1) * GROUP * rows, :], dst_cols[:, wide])
            misfit = 1.0 - counts[part, :, wide].reshape(GROUP * rows, SPAN).astype(F32) / fitted
            hi, lo = split(misfit)
            hi_all[:, wide] = hi
            lo_all[:, wide] = lo
            total = None
            for k in range(GROUP):
                left = fit_cols[s * GROUP + k]
                both = mm(left, hi[k * rows:(k + 1) * rows])
                term = both[:q1] + (both[q1:] + mm(left[:q1], lo[k * rows:(k + 1) * rows]))
                total = term if total is None else total + term
            if s == 0:
                dst_sum[:, wide] = total
            else:
                dst_sum[:, wide] += total
        both = mm(hi_all[...], dst_rows[...])
        through = both[:, :q1] + (both[:, q1:] + mm(lo_all[...], dst_rows[:, :q1]))
        for i in range(GROUP):
            k = s * GROUP + i
            th = halves(through[i * rows:(i + 1) * rows], 1)
            right = halves(core_hours[k].T, 1)
            both = mm(th, jnp.concatenate([right, right], axis=0))
            both = both[:, :p1] + both[:, p1:]
            src_sum = both if src_sum is None else src_sum + both
            both = mm(src_cols, th)
            both = both[:p1] + both[p1:]
            projected[k] = both[:, :q1] + both[:, q1:]
    turned[...] = dst_sum[...].T.reshape(turned.shape)
    src_all[...] = src_sum.reshape(src_all.shape)
    first = 3 + steps
    moves = [(turned.at[lax.rem(x + s, X)], out) for s, out in enumerate((a0, a1, a2, a3))]
    half = hours // CORES
    for mine, out in ((c, own), (1 - c, send)):
        moves.append((projected.at[pl.ds(mine * half, half)], out.at[pl.ds(0, half)]))
        moves.append((src_all.at[pl.ds(mine, 1)], out.at[pl.ds(half, 1)]))
    copies = [pltpu.make_async_copy(a, b, sems.at[first + i]) for i, (a, b) in enumerate(moves)]
    for copy in copies:
        copy.start()
    for copy in copies:
        copy.wait()


def main_call(hour, counts, src, dst, core):
    hours, rows, cols = counts.shape
    rank, p1, q1 = core.shape
    block = cols // X
    half = hours // CORES + 1
    return pl.pallas_call(
        main_kernel,
        out_shape=[struct(block, q1)] * X + [struct(half, p1, q1)] * 2,
        in_specs=[SMEM] + [HBM] * 4,
        out_specs=[HBM] * (X + 2),
        scratch_shapes=[
            pltpu.VMEM(counts.shape, jnp.int32),
            pltpu.VMEM(src.shape, F32),
            pltpu.VMEM(dst.shape, F32),
            pltpu.VMEM(core.shape, F32),
            pltpu.VMEM((hours * rows, 3 * q1), BF16),
            pltpu.VMEM((hours, 2 * q1, rows), BF16),
            pltpu.VMEM((3 * q1, cols), BF16),
            pltpu.VMEM((cols, 2 * q1), BF16),
            pltpu.VMEM((GROUP * rows, cols), BF16),
            pltpu.VMEM((GROUP * rows, cols), BF16),
            pltpu.VMEM((q1, cols), F32),
            pltpu.VMEM((X, block, q1), F32),
            pltpu.VMEM((hours, p1, q1), F32),
            pltpu.VMEM((hours, p1, q1), F32),
            pltpu.VMEM((CORES, rows // CORES, p1), F32),
            pltpu.SemaphoreType.DMA((3 + hours // GROUP + X + 4,)),
        ],
        compiler_params=params(60),
        cost_estimate=cost(2 * 9 * counts.size * q1, 14 << 20),
        name="all_terms",
    )(hour, counts, src, dst, core)


def share_kernel(zs, own, came, core, m0, m1, m2, m3, src_half, rowsums, message):
    half = own.shape[0] - 1
    rank, p1, q1 = core.shape
    x = lax.axis_index("x")
    src_half[...] = own[half] + came[half]
    for k in range(half):
        here = own[k] + came[k]
        for r in range(rank):
            product = (here * core[r]).reshape(p1 // 8, 8, q1)
            at = k * rank + r
            rowsums[at:at + 1, :] = jnp.sum(jnp.sum(product, axis=0), axis=0, keepdims=True)
        for z in range(zs):
            for b in range(X):
                start = (z * X + b) * 4
                row = (z * half + k) * 4
                message[b, row:row + 4, :] = here[start:start + 4]
    sums = jnp.sum(rowsums[...].T, axis=0, keepdims=True)
    tail = jnp.concatenate([sums, jnp.zeros((7, q1), F32)], axis=0)
    size = message.shape[1]
    for s, out in enumerate((m0, m1, m2, m3)):
        out[:size, :] = message[lax.rem(x + s, X)]
        out[size:, :] = tail


def share_call(own, came, core, zs):
    half = own.shape[0] - 1
    rank, p1, q1 = core.shape
    size = half * p1 // X
    return pl.pallas_call(
        functools.partial(share_kernel, zs),
        out_shape=[struct(size + 8, q1)] * X + [struct(p1, q1)],
        in_specs=[VMEM] * 3,
        out_specs=[VMEM] * (X + 1),
        scratch_shapes=[pltpu.VMEM((half * rank, q1), F32), pltpu.VMEM((X, size, q1), F32)],
        compiler_params=params(8),
        cost_estimate=cost(1 << 34, 4 << 20),
        name="hour_terms",
    )(own, came, core)


def small_call(kernel, name, outs, args, flops=1 << 20):
    return pl.pallas_call(
        kernel, out_shape=outs, in_specs=[VMEM] * len(args), out_specs=jax.tree.map(lambda _: VMEM, outs),
        compiler_params=params(4), cost_estimate=cost(flops, 1 << 20), name=name,
    )(*args)


def sum_kernel(*refs):
    parts = [ref[...] for ref in refs[:-1]]
    while len(parts) > 1:
        half = len(parts) // 2
        parts = [a + b for a, b in zip(parts[:half], parts[half:])]
    refs[-1][...] = parts[0]


def summed(name, *parts):
    return small_call(sum_kernel, name, struct(*parts[0].shape), parts)


def x_kernel(a0, a1, a2, a3, m0, m1, m2, m3, out):
    zs, rows, _ = out.shape
    share = a0.shape[0] // zs
    each = rows - share - 8
    a = (a0[...] + a2[...]) + (a1[...] + a3[...])
    m = (m0[...] + m2[...]) + (m1[...] + m3[...])
    for z in range(zs):
        out[z, :share, :] = a[z * share:(z + 1) * share]
        out[z, share:share + each, :] = m[z * each:(z + 1) * each]
        out[z, share + each:, :] = m[zs * each:]


def tail_kernel(share, w, tail):
    tail[...] = jnp.sum(w[:, share:, :], axis=0)


def pair_kernel(own, other, out):
    c = lax.axis_index("core")
    out[c] = own[...]
    out[1 - c] = other[...]


def z_kernel(w, copies):
    share = copies.shape[1]
    total = jnp.sum(w[:, :share, :], axis=0)
    for z in range(copies.shape[0]):
        copies[z] = total


def end_kernel(scales, hour_ref, b0, b1, b2, b3, tails, more, src_own, src_other,
               src_out, dst_out, hour_out, core_out, both):
    x, c = lax.axis_index("x"), lax.axis_index("core")
    src_scale, dst_scale, hour_scale, core_scale = scales
    for s, block in enumerate((b0, b1, b2, b3)):
        dst_out[lax.rem(x - s + X, X)] = block[...] * dst_scale
    src_out[c] = src_own[...] * src_scale
    src_out[1 - c] = src_other[...] * src_scale
    both[...] = tails[...] + more[...]
    hours, rank = hour_ref.shape
    half = hours // CORES
    tiles = []
    for k in range(hours):
        at, i = k // half, k % half
        hour_out[k:k + 1, :] = both[at, 4 * half:4 * half + 1, i * rank:(i + 1) * rank] * hour_scale
        tiles.append(both[at, 4 * i:4 * i + 4, :] * core_scale)
    for r in range(rank):
        out = hour_ref[0, r] * tiles[0]
        for k in range(1, hours):
            out = out + hour_ref[k, r] * tiles[k]
        core_out[r] = out


def end_call(scales, hour, blocks, tails, more, src_own, src_other):
    block, q1 = blocks[0].shape
    hours, rank = hour.shape
    return pl.pallas_call(
        functools.partial(end_kernel, scales),
        in_specs=[SMEM] + [VMEM] * 8,
        out_specs=[VMEM] * 4,
        out_shape=[struct(CORES, *src_own.shape), struct(X, block, q1), struct(hours, rank), struct(rank, 4, q1)],
        scratch_shapes=[pltpu.VMEM(tails.shape, F32)],
        compiler_params=params(8), cost_estimate=cost(1 << 20, 1 << 20), name="outputs",
    )(hour, *blocks, tails, more, src_own, src_other)


def shifted(x, axis, s):
    n = lax.axis_size(axis)
    return lax.ppermute(x, axis, [(i, (i + s) % n) for i in range(n)])


def swapped(x, axis):
    return lax.all_to_all(x, axis, split_axis=0, concat_axis=0, tiled=True)


def paired(x, axis, flip):
    n = lax.axis_size(axis)
    return lax.ppermute(x, axis, [(i, flip(i, n)) for i in range(n)])


def near(i, n):
    return i ^ 1


def far(i, n):
    return n - 1 - i


def around(x, axis):
    return [x] + [shifted(x, axis, s) for s in range(1, lax.axis_size(axis))]


def shards(scales, counts, src_factor, dst_factor, hour_factor, core):
    zs = lax.axis_size("z")
    q1 = dst_factor.shape[1]
    a0, a1, a2, a3, own, send = main_call(hour_factor, counts, src_factor, dst_factor, core)
    a = [a0] + [shifted(v, "x", s) for s, v in ((1, a1), (2, a2), (3, a3))]
    m0, m1, m2, m3, src_half = share_call(own, shifted(send, "core", 1), core, zs)
    m = [m0] + [shifted(v, "x", s) for s, v in ((1, m1), (2, m2), (3, m3))]
    share = a0.shape[0] // zs
    each = (m0.shape[0] - 8) // zs
    src_half, *a = lax.optimization_barrier((src_half, *a))
    src_half = summed("src_near_sum", src_half, paired(src_half, "y", near))
    m, src_half = lax.optimization_barrier((m, src_half))
    w = small_call(x_kernel, "x_sums", struct(zs, share + each + 8, q1), [*a, *m])
    w = swapped(w, "z")
    src_half = summed("src_far_sum", src_half, paired(src_half, "y", far))
    w, src_half = lax.optimization_barrier((w, src_half))
    src_other = shifted(src_half, "core", 1)
    tail = small_call(functools.partial(tail_kernel, share), "tail_sums", struct(each + 8, q1), [w])
    copies = small_call(z_kernel, "z_sums", struct(zs, share, q1), [w])
    tails = small_call(pair_kernel, "both_tails", struct(CORES, *tail.shape), [tail, shifted(tail, "core", 1)])
    tails = summed("near_sum", tails, paired(tails, "y", near))
    block = swapped(copies, "z").reshape(zs * share, q1)
    block, tails = lax.optimization_barrier((block, tails))
    more = paired(tails, "y", far)
    blocks = around(block, "x")
    grad_src, grad_dst, grad_hour, grad_core = end_call(
        scales, hour_factor, blocks, tails, more, src_half, src_other)
    return (grad_src.reshape(src_factor.shape), grad_dst.reshape(dst_factor.shape), grad_hour, grad_core)


def solution(mesh):
    n_src, n_dst = mesh.shape["src"], mesh.shape["dst"]
    fine = Mesh(mesh.devices.reshape(n_src // X, X, n_dst // CORES, CORES), ("z", "x", "y", "core"))
    src, dst = ("z", "x"), ("y", "core")
    in_specs = (P(None, src, dst), P(src, None), P(dst, None), P(), P())
    out_specs = (P(src, None), P(dst, None), P(), P(None, src, None))

    def run(counts, src_factor, dst_factor, hour_factor, core):
        hours, total_src, total_dst = counts.shape
        scales = (1 / math.sqrt(total_dst * hours), 1 / math.sqrt(total_src * hours),
                  1 / math.sqrt(total_src * total_dst), 1 / math.sqrt(total_src * total_dst * hours))
        body = jax.shard_map(functools.partial(shards, scales), mesh=fine, in_specs=in_specs,
                             out_specs=out_specs, check_vma=False)
        return body(counts, src_factor, dst_factor, hour_factor, core)

    return run
```

```python
import functools
import math

import jax
import jax.numpy as jnp
from jax import lax
from jax.experimental import pallas as pl
from jax.experimental.pallas import tpu as pltpu
from jax.sharding import Mesh, PartitionSpec as P

X = 4
CORES = 2
GROUP = 4
SPAN = 512
F32 = jnp.float32
BF16 = jnp.bfloat16
HBM = pl.BlockSpec(memory_space=pltpu.HBM)
VMEM = pl.BlockSpec(memory_space=pltpu.VMEM)
SMEM = pl.BlockSpec(memory_space=pltpu.SMEM)


def struct(*shape, dtype=F32):
    return jax.ShapeDtypeStruct(shape, dtype)


def params(mib):
    return pltpu.CompilerParams(vmem_limit_bytes=mib << 20)


def cost(flops, size):
    return pl.CostEstimate(flops=flops, bytes_accessed=size, transcendentals=0)


def split(x):
    hi = x.astype(BF16)
    return hi, (x - hi.astype(F32)).astype(BF16)


def mm(a, b):
    return jnp.dot(a, b, preferred_element_type=F32)


def halves(x, axis):
    return jnp.concatenate(split(x), axis=axis)


def main_kernel(hour_ref, counts_hbm, src_hbm, dst_hbm, core_hbm,
                a0, a1, a2, a3, own, send,
                counts, src, dst, core, fit_rows, fit_cols, dst_cols, dst_rows, hi_all, lo_all, dst_sum, turned,
                core_hours, projected, src_all, sems):
    hours, rows, cols = counts.shape
    rank, p1, q1 = core.shape
    steps = hours // GROUP
    x, c = lax.axis_index("x"), lax.axis_index("core")
    small = [pltpu.make_async_copy(a, b, sems.at[i])
             for i, (a, b) in enumerate(((core_hbm, core), (src_hbm, src), (dst_hbm, dst)))]
    parts = [pl.ds(s * GROUP, GROUP) for s in range(steps)]
    large = [pltpu.make_async_copy(counts_hbm.at[part], counts.at[part], sems.at[3 + s])
             for s, part in enumerate(parts)]
    for copy in small[::-1] + large:
        copy.start()
    small[2].wait()
    dst_rows[...] = halves(dst[...], 1)
    hi, lo = split(dst[...].T)
    dst_cols[...] = jnp.concatenate([hi, hi, lo], axis=0)
    small[0].wait()
    small[1].wait()
    hi, lo = split(src[...])
    src_rows = jnp.concatenate([hi, lo, hi], axis=1)
    for k in range(hours):
        core_hour = hour_ref[k, 0] * core[0]
        for r in range(1, rank):
            core_hour = core_hour + hour_ref[k, r] * core[r]
        core_hours[k] = core_hour
        hi, lo = split(core_hour)
        fit = mm(src_rows, jnp.concatenate([hi, hi, lo], axis=0))
        hi, lo = split(fit)
        fit_rows[k * rows:(k + 1) * rows] = jnp.concatenate([hi, lo, hi], axis=1)
        fit_cols[k] = halves(fit.T, 0)
    src_cols = halves(src[...].T, 0)
    src_sum = None
    for s, part in enumerate(parts):
        large[s].wait()
        for j in range(0, cols, SPAN):
            wide = pl.ds(j, SPAN)
            fitted = mm(fit_rows[s * GROUP * rows:(s + 1) * GROUP * rows, :], dst_cols[:, wide])
            misfit = 1.0 - counts[part, :, wide].reshape(GROUP * rows, SPAN).astype(F32) / fitted
            hi, lo = split(misfit)
            hi_all[:, wide] = hi
            lo_all[:, wide] = lo
            total = None
            for k in range(GROUP):
                left = fit_cols[s * GROUP + k]
                both = mm(left, hi[k * rows:(k + 1) * rows])
                term = both[:q1] + (both[q1:] + mm(left[:q1], lo[k * rows:(k + 1) * rows]))
                total = term if total is None else total + term
            if s == 0:
                dst_sum[:, wide] = total
            else:
                dst_sum[:, wide] += total
        both = mm(hi_all[...], dst_rows[...])
        through = both[:, :q1] + (both[:, q1:] + mm(lo_all[...], dst_rows[:, :q1]))
        for i in range(GROUP):
            k = s * GROUP + i
            th = halves(through[i * rows:(i + 1) * rows], 1)
            right = halves(core_hours[k].T, 1)
            both = mm(th, jnp.concatenate([right, right], axis=0))
            both = both[:, :p1] + both[:, p1:]
            src_sum = both if src_sum is None else src_sum + both
            both = mm(src_cols, th)
            both = both[:p1] + both[p1:]
            projected[k] = both[:, :q1] + both[:, q1:]
    turned[...] = dst_sum[...].T.reshape(turned.shape)
    src_all[...] = src_sum.reshape(src_all.shape)
    first = 3 + steps
    moves = [(turned.at[lax.rem(x + s, X)], out) for s, out in enumerate((a0, a1, a2, a3))]
    half = hours // CORES
    for mine, out in ((c, own), (1 - c, send)):
        moves.append((projected.at[pl.ds(mine * half, half)], out.at[pl.ds(0, half)]))
        moves.append((src_all.at[pl.ds(mine, 1)], out.at[pl.ds(half, 1)]))
    copies = [pltpu.make_async_copy(a, b, sems.at[first + i]) for i, (a, b) in enumerate(moves)]
    for copy in copies:
        copy.start()
    for copy in copies:
        copy.wait()


def main_call(hour, counts, src, dst, core):
    hours, rows, cols = counts.shape
    rank, p1, q1 = core.shape
    block = cols // X
    half = hours // CORES + 1
    return pl.pallas_call(
        main_kernel,
        out_shape=[struct(block, q1)] * X + [struct(half, p1, q1)] * 2,
        in_specs=[SMEM] + [HBM] * 4,
        out_specs=[HBM] * (X + 2),
        scratch_shapes=[
            pltpu.VMEM(counts.shape, jnp.int32),
            pltpu.VMEM(src.shape, F32),
            pltpu.VMEM(dst.shape, F32),
            pltpu.VMEM(core.shape, F32),
            pltpu.VMEM((hours * rows, 3 * q1), BF16),
            pltpu.VMEM((hours, 2 * q1, rows), BF16),
            pltpu.VMEM((3 * q1, cols), BF16),
            pltpu.VMEM((cols, 2 * q1), BF16),
            pltpu.VMEM((GROUP * rows, cols), BF16),
            pltpu.VMEM((GROUP * rows, cols), BF16),
            pltpu.VMEM((q1, cols), F32),
            pltpu.VMEM((X, block, q1), F32),
            pltpu.VMEM((hours, p1, q1), F32),
            pltpu.VMEM((hours, p1, q1), F32),
            pltpu.VMEM((CORES, rows // CORES, p1), F32),
            pltpu.SemaphoreType.DMA((3 + hours // GROUP + X + 4,)),
        ],
        compiler_params=params(60),
        cost_estimate=cost(2 * 9 * counts.size * q1, 14 << 20),
        name="all_terms",
    )(hour, counts, src, dst, core)


def share_kernel(zs, own, came, core, m0, m1, m2, m3, src_half, rowsums, message):
    half = own.shape[0] - 1
    rank, p1, q1 = core.shape
    x = lax.axis_index("x")
    src_half[...] = own[half] + came[half]
    for k in range(half):
        here = own[k] + came[k]
        for r in range(rank):
            product = (here * core[r]).reshape(p1 // 8, 8, q1)
            at = k * rank + r
            rowsums[at:at + 1, :] = jnp.sum(jnp.sum(product, axis=0), axis=0, keepdims=True)
        for z in range(zs):
            for b in range(X):
                start = (z * X + b) * 4
                row = (z * half + k) * 4
                message[b, row:row + 4, :] = here[start:start + 4]
    sums = jnp.sum(rowsums[...].T, axis=0, keepdims=True)
    tail = jnp.concatenate([sums, jnp.zeros((7, q1), F32)], axis=0)
    size = message.shape[1]
    for s, out in enumerate((m0, m1, m2, m3)):
        out[:size, :] = message[lax.rem(x + s, X)]
        out[size:, :] = tail


def share_call(own, came, core, zs):
    half = own.shape[0] - 1
    rank, p1, q1 = core.shape
    size = half * p1 // X
    return pl.pallas_call(
        functools.partial(share_kernel, zs),
        out_shape=[struct(size + 8, q1)] * X + [struct(p1, q1)],
        in_specs=[VMEM] * 3,
        out_specs=[VMEM] * (X + 1),
        scratch_shapes=[pltpu.VMEM((half * rank, q1), F32), pltpu.VMEM((X, size, q1), F32)],
        compiler_params=params(8),
        cost_estimate=cost(1 << 34, 4 << 20),
        name="hour_terms",
    )(own, came, core)


def small_call(kernel, name, outs, args, flops=1 << 20):
    return pl.pallas_call(
        kernel, out_shape=outs, in_specs=[VMEM] * len(args), out_specs=jax.tree.map(lambda _: VMEM, outs),
        compiler_params=params(4), cost_estimate=cost(flops, 1 << 20), name=name,
    )(*args)


def sum_kernel(*refs):
    parts = [ref[...] for ref in refs[:-1]]
    while len(parts) > 1:
        half = len(parts) // 2
        parts = [a + b for a, b in zip(parts[:half], parts[half:])]
    refs[-1][...] = parts[0]


def summed(name, *parts):
    return small_call(sum_kernel, name, struct(*parts[0].shape), parts)


def x_kernel(a0, a1, a2, a3, m0, m1, m2, m3, out):
    zs, rows, _ = out.shape
    share = a0.shape[0] // zs
    each = rows - share - 8
    a = (a0[...] + a2[...]) + (a1[...] + a3[...])
    m = (m0[...] + m2[...]) + (m1[...] + m3[...])
    for z in range(zs):
        out[z, :share, :] = a[z * share:(z + 1) * share]
        out[z, share:share + each, :] = m[z * each:(z + 1) * each]
        out[z, share + each:, :] = m[zs * each:]


def tail_kernel(share, w, tail):
    tail[...] = jnp.sum(w[:, share:, :], axis=0)


def pair_kernel(own, other, out):
    c = lax.axis_index("core")
    out[c] = own[...]
    out[1 - c] = other[...]


def scaled_sum_kernel(scale, a, b, out):
    out[...] = (a[...] + b[...]) * scale


def z_kernel(scale, w, copies):
    share = copies.shape[1]
    total = jnp.sum(w[:, :share, :], axis=0) * scale
    for z in range(copies.shape[0]):
        copies[z] = total


def end_kernel(scales, hour_ref, b0, b1, b2, b3, tails, more, src_own, src_other,
               src_out, dst_out, hour_out, core_out, both, sems):
    x, c = lax.axis_index("x"), lax.axis_index("core")
    hour_scale, core_scale = scales
    moves = [(block, dst_out.at[lax.rem(x - s + X, X)]) for s, block in enumerate((b0, b1, b2, b3))]
    moves += [(src_own, src_out.at[c]), (src_other, src_out.at[1 - c])]
    copies = [pltpu.make_async_copy(a, b, sems.at[i]) for i, (a, b) in enumerate(moves)]
    for copy in copies:
        copy.start()
    both[...] = tails[...] + more[...]
    hours, rank = hour_ref.shape
    half = hours // CORES
    tiles = []
    for k in range(hours):
        at, i = k // half, k % half
        hour_out[k:k + 1, :] = both[at, 4 * half:4 * half + 1, i * rank:(i + 1) * rank] * hour_scale
        tiles.append(both[at, 4 * i:4 * i + 4, :] * core_scale)
    for r in range(rank):
        out = hour_ref[0, r] * tiles[0]
        for k in range(1, hours):
            out = out + hour_ref[k, r] * tiles[k]
        core_out[r] = out
    for copy in copies:
        copy.wait()


def end_call(scales, hour, blocks, tails, more, src_own, src_other):
    block, q1 = blocks[0].shape
    hours, rank = hour.shape
    return pl.pallas_call(
        functools.partial(end_kernel, scales),
        in_specs=[SMEM] + [VMEM] * 8,
        out_specs=[HBM] * 2 + [VMEM] * 2,
        out_shape=[struct(CORES, *src_own.shape), struct(X, block, q1), struct(hours, rank), struct(rank, 4, q1)],
        scratch_shapes=[pltpu.VMEM(tails.shape, F32), pltpu.SemaphoreType.DMA((X + CORES,))],
        compiler_params=params(8), cost_estimate=cost(1 << 20, 1 << 20), name="outputs",
    )(hour, *blocks, tails, more, src_own, src_other)


def shifted(x, axis, s):
    n = lax.axis_size(axis)
    return lax.ppermute(x, axis, [(i, (i + s) % n) for i in range(n)])


def swapped(x, axis):
    return lax.all_to_all(x, axis, split_axis=0, concat_axis=0, tiled=True)


def paired(x, axis, flip):
    n = lax.axis_size(axis)
    return lax.ppermute(x, axis, [(i, flip(i, n)) for i in range(n)])


def near(i, n):
    return i ^ 1


def far(i, n):
    return n - 1 - i


def around(x, axis):
    return [x] + [shifted(x, axis, s) for s in range(1, lax.axis_size(axis))]


def shards(scales, counts, src_factor, dst_factor, hour_factor, core):
    zs = lax.axis_size("z")
    q1 = dst_factor.shape[1]
    a0, a1, a2, a3, own, send = main_call(hour_factor, counts, src_factor, dst_factor, core)
    a = [a0] + [shifted(v, "x", s) for s, v in ((1, a1), (2, a2), (3, a3))]
    m0, m1, m2, m3, src_half = share_call(own, shifted(send, "core", 1), core, zs)
    m = [m0] + [shifted(v, "x", s) for s, v in ((1, m1), (2, m2), (3, m3))]
    share = a0.shape[0] // zs
    each = (m0.shape[0] - 8) // zs
    src_half, *a = lax.optimization_barrier((src_half, *a))
    src_half = summed("src_near_sum", src_half, paired(src_half, "y", near))
    m, src_half = lax.optimization_barrier((m, src_half))
    w = small_call(x_kernel, "x_sums", struct(zs, share + each + 8, q1), [*a, *m])
    w = swapped(w, "z")
    src_half = small_call(functools.partial(scaled_sum_kernel, scales[0]), "src_far_sum",
                          struct(*src_half.shape), [src_half, paired(src_half, "y", far)])
    w, src_half = lax.optimization_barrier((w, src_half))
    src_other = shifted(src_half, "core", 1)
    tail = small_call(functools.partial(tail_kernel, share), "tail_sums", struct(each + 8, q1), [w])
    copies = small_call(functools.partial(z_kernel, scales[1]), "z_sums", struct(zs, share, q1), [w])
    copies, other = lax.optimization_barrier((copies, shifted(tail, "core", 1)))
    tails = small_call(pair_kernel, "both_tails", struct(CORES, *tail.shape), [tail, other])
    tails = summed("near_sum", tails, paired(tails, "y", near))
    block = swapped(copies, "z").reshape(zs * share, q1)
    block, tails = lax.optimization_barrier((block, tails))
    more = paired(tails, "y", far)
    blocks = around(block, "x")
    grad_src, grad_dst, grad_hour, grad_core = end_call(
        scales[2:], hour_factor, blocks, tails, more, src_half, src_other)
    return (grad_src.reshape(src_factor.shape), grad_dst.reshape(dst_factor.shape), grad_hour, grad_core)


def solution(mesh):
    n_src, n_dst = mesh.shape["src"], mesh.shape["dst"]
    fine = Mesh(mesh.devices.reshape(n_src // X, X, n_dst // CORES, CORES), ("z", "x", "y", "core"))
    src, dst = ("z", "x"), ("y", "core")
    in_specs = (P(None, src, dst), P(src, None), P(dst, None), P(), P())
    out_specs = (P(src, None), P(dst, None), P(), P(None, src, None))

    def run(counts, src_factor, dst_factor, hour_factor, core):
        hours, total_src, total_dst = counts.shape
        scales = (1 / math.sqrt(total_dst * hours), 1 / math.sqrt(total_src * hours),
                  1 / math.sqrt(total_src * total_dst), 1 / math.sqrt(total_src * total_dst * hours))
        body = jax.shard_map(functools.partial(shards, scales), mesh=fine, in_specs=in_specs,
                             out_specs=out_specs, check_vma=False)
        return body(counts, src_factor, dst_factor, hour_factor, core)

    return run
```

```python
import functools
import math

import jax
import jax.numpy as jnp
from jax import lax
from jax.experimental import pallas as pl
from jax.experimental.pallas import tpu as pltpu
from jax.sharding import Mesh, PartitionSpec as P

X = 4
CORES = 2
GROUP = 4
SPAN = 512
F32 = jnp.float32
BF16 = jnp.bfloat16
HBM = pl.BlockSpec(memory_space=pltpu.HBM)
VMEM = pl.BlockSpec(memory_space=pltpu.VMEM)
SMEM = pl.BlockSpec(memory_space=pltpu.SMEM)


def struct(*shape, dtype=F32):
    return jax.ShapeDtypeStruct(shape, dtype)


def params(mib):
    return pltpu.CompilerParams(vmem_limit_bytes=mib << 20)


def cost(flops, size):
    return pl.CostEstimate(flops=flops, bytes_accessed=size, transcendentals=0)


def split(x):
    hi = x.astype(BF16)
    return hi, (x - hi.astype(F32)).astype(BF16)


def mm(a, b):
    return jnp.dot(a, b, preferred_element_type=F32)


def halves(x, axis):
    return jnp.concatenate(split(x), axis=axis)


def main_kernel(hour_ref, counts_hbm, src_hbm, dst_hbm, core_hbm,
                a0, a1, a2, a3, own, send,
                counts, src, dst, core, fit_rows, fit_cols, dst_cols, dst_rows, hi_all, lo_all, dst_sum, turned,
                core_hours, projected, src_all, sems):
    hours, rows, cols = counts.shape
    rank, p1, q1 = core.shape
    steps = hours // GROUP
    x, c = lax.axis_index("x"), lax.axis_index("core")
    small = [pltpu.make_async_copy(a, b, sems.at[i])
             for i, (a, b) in enumerate(((core_hbm, core), (src_hbm, src), (dst_hbm, dst)))]
    parts = [pl.ds(s * GROUP, GROUP) for s in range(steps)]
    large = [pltpu.make_async_copy(counts_hbm.at[part], counts.at[part], sems.at[3 + s])
             for s, part in enumerate(parts)]
    for copy in small[::-1] + large:
        copy.start()
    small[2].wait()
    dst_rows[...] = halves(dst[...], 1)
    hi, lo = split(dst[...].T)
    dst_cols[...] = jnp.concatenate([hi, hi, lo], axis=0)
    small[0].wait()
    small[1].wait()
    hi, lo = split(src[...])
    src_rows = jnp.concatenate([hi, lo, hi], axis=1)
    for k in range(hours):
        core_hour = hour_ref[k, 0] * core[0]
        for r in range(1, rank):
            core_hour = core_hour + hour_ref[k, r] * core[r]
        core_hours[k] = core_hour
        hi, lo = split(core_hour)
        fit = mm(src_rows, jnp.concatenate([hi, hi, lo], axis=0))
        hi, lo = split(fit)
        fit_rows[k * rows:(k + 1) * rows] = jnp.concatenate([hi, lo, hi], axis=1)
        fit_cols[k] = halves(fit.T, 0)
    src_cols = halves(src[...].T, 0)
    src_sum = None
    for s, part in enumerate(parts):
        large[s].wait()
        for j in range(0, cols, SPAN):
            wide = pl.ds(j, SPAN)
            fitted = mm(fit_rows[s * GROUP * rows:(s + 1) * GROUP * rows, :], dst_cols[:, wide])
            misfit = 1.0 - counts[part, :, wide].reshape(GROUP * rows, SPAN).astype(F32) / fitted
            hi, lo = split(misfit)
            hi_all[:, wide] = hi
            lo_all[:, wide] = lo
            total = None
            for k in range(GROUP):
                left = fit_cols[s * GROUP + k]
                both = mm(left, hi[k * rows:(k + 1) * rows])
                term = both[:q1] + (both[q1:] + mm(left[:q1], lo[k * rows:(k + 1) * rows]))
                total = term if total is None else total + term
            if s == 0:
                dst_sum[:, wide] = total
            else:
                dst_sum[:, wide] += total
        both = mm(hi_all[...], dst_rows[...])
        through = both[:, :q1] + (both[:, q1:] + mm(lo_all[...], dst_rows[:, :q1]))
        for i in range(GROUP):
            k = s * GROUP + i
            th = halves(through[i * rows:(i + 1) * rows], 1)
            right = halves(core_hours[k].T, 1)
            both = mm(th, jnp.concatenate([right, right], axis=0))
            both = both[:, :p1] + both[:, p1:]
            src_sum = both if src_sum is None else src_sum + both
            both = mm(src_cols, th)
            both = both[:p1] + both[p1:]
            projected[k] = both[:, :q1] + both[:, q1:]
    turned[...] = dst_sum[...].T.reshape(turned.shape)
    src_all[...] = src_sum.reshape(src_all.shape)
    first = 3 + steps
    moves = [(turned.at[lax.rem(x + s, X)], out) for s, out in enumerate((a0, a1, a2, a3))]
    half = hours // CORES
    for mine, out in ((c, own), (1 - c, send)):
        moves.append((projected.at[pl.ds(mine * half, half)], out.at[pl.ds(0, half)]))
        moves.append((src_all.at[pl.ds(mine, 1)], out.at[pl.ds(half, 1)]))
    copies = [pltpu.make_async_copy(a, b, sems.at[first + i]) for i, (a, b) in enumerate(moves)]
    for copy in copies:
        copy.start()
    for copy in copies:
        copy.wait()


def main_call(hour, counts, src, dst, core):
    hours, rows, cols = counts.shape
    rank, p1, q1 = core.shape
    block = cols // X
    half = hours // CORES + 1
    return pl.pallas_call(
        main_kernel,
        out_shape=[struct(block, q1)] * X + [struct(half, p1, q1)] * 2,
        in_specs=[SMEM] + [HBM] * 4,
        out_specs=[HBM] * (X + 2),
        scratch_shapes=[
            pltpu.VMEM(counts.shape, jnp.int32),
            pltpu.VMEM(src.shape, F32),
            pltpu.VMEM(dst.shape, F32),
            pltpu.VMEM(core.shape, F32),
            pltpu.VMEM((hours * rows, 3 * q1), BF16),
            pltpu.VMEM((hours, 2 * q1, rows), BF16),
            pltpu.VMEM((3 * q1, cols), BF16),
            pltpu.VMEM((cols, 2 * q1), BF16),
            pltpu.VMEM((GROUP * rows, cols), BF16),
            pltpu.VMEM((GROUP * rows, cols), BF16),
            pltpu.VMEM((q1, cols), F32),
            pltpu.VMEM((X, block, q1), F32),
            pltpu.VMEM((hours, p1, q1), F32),
            pltpu.VMEM((hours, p1, q1), F32),
            pltpu.VMEM((CORES, rows // CORES, p1), F32),
            pltpu.SemaphoreType.DMA((3 + hours // GROUP + X + 4,)),
        ],
        compiler_params=params(60),
        cost_estimate=cost(2 * 9 * counts.size * q1, 14 << 20),
        name="all_terms",
    )(hour, counts, src, dst, core)


def share_kernel(zs, own, came, core, m0, m1, m2, m3, src_half, rowsums, message):
    half = own.shape[0] - 1
    rank, p1, q1 = core.shape
    x = lax.axis_index("x")
    src_half[...] = own[half] + came[half]
    for k in range(half):
        here = own[k] + came[k]
        for r in range(rank):
            product = (here * core[r]).reshape(p1 // 8, 8, q1)
            at = k * rank + r
            rowsums[at:at + 1, :] = jnp.sum(jnp.sum(product, axis=0), axis=0, keepdims=True)
        for z in range(zs):
            for b in range(X):
                start = (z * X + b) * 4
                row = (z * half + k) * 4
                message[b, row:row + 4, :] = here[start:start + 4]
    sums = jnp.sum(rowsums[...].T, axis=0, keepdims=True)
    tail = jnp.concatenate([sums, jnp.zeros((7, q1), F32)], axis=0)
    size = message.shape[1]
    for s, out in enumerate((m0, m1, m2, m3)):
        out[:size, :] = message[lax.rem(x + s, X)]
        out[size:, :] = tail


def share_call(own, came, core, zs):
    half = own.shape[0] - 1
    rank, p1, q1 = core.shape
    size = half * p1 // X
    return pl.pallas_call(
        functools.partial(share_kernel, zs),
        out_shape=[struct(size + 8, q1)] * X + [struct(p1, q1)],
        in_specs=[VMEM] * 3,
        out_specs=[VMEM] * (X + 1),
        scratch_shapes=[pltpu.VMEM((half * rank, q1), F32), pltpu.VMEM((X, size, q1), F32)],
        compiler_params=params(8),
        cost_estimate=cost(1 << 34, 4 << 20),
        name="hour_terms",
    )(own, came, core)


def small_call(kernel, name, outs, args, flops=1 << 20):
    return pl.pallas_call(
        kernel, out_shape=outs, in_specs=[VMEM] * len(args), out_specs=jax.tree.map(lambda _: VMEM, outs),
        compiler_params=params(4), cost_estimate=cost(flops, 1 << 20), name=name,
    )(*args)


def sum_kernel(*refs):
    parts = [ref[...] for ref in refs[:-1]]
    while len(parts) > 1:
        half = len(parts) // 2
        parts = [a + b for a, b in zip(parts[:half], parts[half:])]
    refs[-1][...] = parts[0]


def summed(name, *parts):
    return small_call(sum_kernel, name, struct(*parts[0].shape), parts)


def x_kernel(a0, a1, a2, a3, m0, m1, m2, m3, out):
    zs, rows, _ = out.shape
    share = a0.shape[0] // zs
    each = rows - share - 8
    a = (a0[...] + a2[...]) + (a1[...] + a3[...])
    m = (m0[...] + m2[...]) + (m1[...] + m3[...])
    for z in range(zs):
        out[z, :share, :] = a[z * share:(z + 1) * share]
        out[z, share:share + each, :] = m[z * each:(z + 1) * each]
        out[z, share + each:, :] = m[zs * each:]


def tail_kernel(share, w, tail):
    tail[...] = jnp.sum(w[:, share:, :], axis=0)


def pair_kernel(own, other, out):
    c = lax.axis_index("core")
    out[c] = own[...]
    out[1 - c] = other[...]


def z_kernel(w, copies):
    share = copies.shape[1]
    total = jnp.sum(w[:, :share, :], axis=0)
    for z in range(copies.shape[0]):
        copies[z] = total


def end_kernel(scales, hour_ref, b0, b1, b2, b3, tails, more, src_own, src_other,
               src_out, dst_out, hour_out, core_out, both):
    x, c = lax.axis_index("x"), lax.axis_index("core")
    src_scale, dst_scale, hour_scale, core_scale = scales
    for s, block in enumerate((b0, b1, b2, b3)):
        dst_out[lax.rem(x - s + X, X)] = block[...] * dst_scale
    src_out[c] = src_own[...] * src_scale
    src_out[1 - c] = src_other[...] * src_scale
    both[...] = tails[...] + more[...]
    hours, rank = hour_ref.shape
    half = hours // CORES
    tiles = []
    for k in range(hours):
        at, i = k // half, k % half
        hour_out[k:k + 1, :] = both[at, 4 * half:4 * half + 1, i * rank:(i + 1) * rank] * hour_scale
        tiles.append(both[at, 4 * i:4 * i + 4, :] * core_scale)
    for r in range(rank):
        out = hour_ref[0, r] * tiles[0]
        for k in range(1, hours):
            out = out + hour_ref[k, r] * tiles[k]
        core_out[r] = out


def end_call(scales, hour, blocks, tails, more, src_own, src_other):
    block, q1 = blocks[0].shape
    hours, rank = hour.shape
    return pl.pallas_call(
        functools.partial(end_kernel, scales),
        in_specs=[SMEM] + [VMEM] * 8,
        out_specs=[VMEM] * 4,
        out_shape=[struct(CORES, *src_own.shape), struct(X, block, q1), struct(hours, rank), struct(rank, 4, q1)],
        scratch_shapes=[pltpu.VMEM(tails.shape, F32)],
        compiler_params=params(8), cost_estimate=cost(1 << 20, 1 << 20), name="outputs",
    )(hour, *blocks, tails, more, src_own, src_other)


def shifted(x, axis, s):
    n = lax.axis_size(axis)
    return lax.ppermute(x, axis, [(i, (i + s) % n) for i in range(n)])


def swapped(x, axis):
    return lax.all_to_all(x, axis, split_axis=0, concat_axis=0, tiled=True)


def paired(x, axis, flip):
    n = lax.axis_size(axis)
    return lax.ppermute(x, axis, [(i, flip(i, n)) for i in range(n)])


def near(i, n):
    return i ^ 1


def far(i, n):
    return n - 1 - i


def around(x, axis):
    return [x] + [shifted(x, axis, s) for s in range(1, lax.axis_size(axis))]


def shards(scales, counts, src_factor, dst_factor, hour_factor, core):
    zs = lax.axis_size("z")
    q1 = dst_factor.shape[1]
    a0, a1, a2, a3, own, send = main_call(hour_factor, counts, src_factor, dst_factor, core)
    a = [a0] + [shifted(v, "x", s) for s, v in ((1, a1), (2, a2), (3, a3))]
    m0, m1, m2, m3, src_half = share_call(own, shifted(send, "core", 1), core, zs)
    m = [m0] + [shifted(v, "x", s) for s, v in ((1, m1), (2, m2), (3, m3))]
    share = a0.shape[0] // zs
    each = (m0.shape[0] - 8) // zs
    src_half, a[1], a[2] = lax.optimization_barrier((src_half, a[1], a[2]))
    src_half = summed("src_near_sum", src_half, paired(src_half, "y", near))
    m, src_half = lax.optimization_barrier((m, src_half))
    w = small_call(x_kernel, "x_sums", struct(zs, share + each + 8, q1), [*a, *m])
    w = swapped(w, "z")
    src_half = summed("src_far_sum", src_half, paired(src_half, "y", far))
    src_other = shifted(src_half, "core", 1)
    w, src_half, src_other = lax.optimization_barrier((w, src_half, src_other))
    tail = small_call(functools.partial(tail_kernel, share), "tail_sums", struct(each + 8, q1), [w])
    copies = small_call(z_kernel, "z_sums", struct(zs, share, q1), [w])
    tails = small_call(pair_kernel, "both_tails", struct(CORES, *tail.shape), [tail, shifted(tail, "core", 1)])
    tails = summed("near_sum", tails, paired(tails, "y", near))
    block = swapped(copies, "z").reshape(zs * share, q1)
    block, tails = lax.optimization_barrier((block, tails))
    more = paired(tails, "y", far)
    blocks = around(block, "x")
    grad_src, grad_dst, grad_hour, grad_core = end_call(
        scales, hour_factor, blocks, tails, more, src_half, src_other)
    return (grad_src.reshape(src_factor.shape), grad_dst.reshape(dst_factor.shape), grad_hour, grad_core)


def solution(mesh):
    n_src, n_dst = mesh.shape["src"], mesh.shape["dst"]
    fine = Mesh(mesh.devices.reshape(n_src // X, X, n_dst // CORES, CORES), ("z", "x", "y", "core"))
    src, dst = ("z", "x"), ("y", "core")
    in_specs = (P(None, src, dst), P(src, None), P(dst, None), P(), P())
    out_specs = (P(src, None), P(dst, None), P(), P(None, src, None))

    def run(counts, src_factor, dst_factor, hour_factor, core):
        hours, total_src, total_dst = counts.shape
        scales = (1 / math.sqrt(total_dst * hours), 1 / math.sqrt(total_src * hours),
                  1 / math.sqrt(total_src * total_dst), 1 / math.sqrt(total_src * total_dst * hours))
        body = jax.shard_map(functools.partial(shards, scales), mesh=fine, in_specs=in_specs,
                             out_specs=out_specs, check_vma=False)
        return body(counts, src_factor, dst_factor, hour_factor, core)

    return run
```

```python
import functools
import math

import jax
import jax.numpy as jnp
from jax import lax
from jax.experimental import pallas as pl
from jax.experimental.pallas import tpu as pltpu
from jax.sharding import Mesh, PartitionSpec as P

X = 4
CORES = 2
GROUP = 4
SPAN = 512
F32 = jnp.float32
BF16 = jnp.bfloat16
HBM = pl.BlockSpec(memory_space=pltpu.HBM)
VMEM = pl.BlockSpec(memory_space=pltpu.VMEM)
SMEM = pl.BlockSpec(memory_space=pltpu.SMEM)


def struct(*shape, dtype=F32):
    return jax.ShapeDtypeStruct(shape, dtype)


def params(mib):
    return pltpu.CompilerParams(vmem_limit_bytes=mib << 20)


def cost(flops, size):
    return pl.CostEstimate(flops=flops, bytes_accessed=size, transcendentals=0)


def split(x):
    hi = x.astype(BF16)
    return hi, (x - hi.astype(F32)).astype(BF16)


def mm(a, b):
    return jnp.dot(a, b, preferred_element_type=F32)


def halves(x, axis):
    return jnp.concatenate(split(x), axis=axis)


def main_kernel(hour_ref, counts_hbm, src_hbm, dst_hbm, core_hbm,
                a0, a1, a2, a3, own, send,
                counts, src, dst, core, fit_rows, fit_cols, dst_cols, dst_rows, hi_all, lo_all, dst_sum, turned,
                core_hours, projected, src_all, sems):
    hours, rows, cols = counts.shape
    rank, p1, q1 = core.shape
    steps = hours // GROUP
    x, c = lax.axis_index("x"), lax.axis_index("core")
    small = [pltpu.make_async_copy(a, b, sems.at[i])
             for i, (a, b) in enumerate(((core_hbm, core), (src_hbm, src), (dst_hbm, dst)))]
    parts = [pl.ds(s * GROUP, GROUP) for s in range(steps)]
    large = [pltpu.make_async_copy(counts_hbm.at[part], counts.at[part], sems.at[3 + s])
             for s, part in enumerate(parts)]
    for copy in small[::-1] + large:
        copy.start()
    small[2].wait()
    dst_rows[...] = halves(dst[...], 1)
    hi, lo = split(dst[...].T)
    dst_cols[...] = jnp.concatenate([hi, hi, lo], axis=0)
    small[0].wait()
    small[1].wait()
    hi, lo = split(src[...])
    src_rows = jnp.concatenate([hi, lo, hi], axis=1)
    for k in range(hours):
        core_hour = hour_ref[k, 0] * core[0]
        for r in range(1, rank):
            core_hour = core_hour + hour_ref[k, r] * core[r]
        core_hours[k] = core_hour
        hi, lo = split(core_hour)
        fit = mm(src_rows, jnp.concatenate([hi, hi, lo], axis=0))
        hi, lo = split(fit)
        fit_rows[k * rows:(k + 1) * rows] = jnp.concatenate([hi, lo, hi], axis=1)
        fit_cols[k] = halves(fit.T, 0)
    src_cols = halves(src[...].T, 0)
    src_sum = None
    for s, part in enumerate(parts):
        large[s].wait()
        for j in range(0, cols, SPAN):
            wide = pl.ds(j, SPAN)
            fitted = mm(fit_rows[s * GROUP * rows:(s + 1) * GROUP * rows, :], dst_cols[:, wide])
            misfit = 1.0 - counts[part, :, wide].reshape(GROUP * rows, SPAN).astype(F32) / fitted
            hi, lo = split(misfit)
            hi_all[:, wide] = hi
            lo_all[:, wide] = lo
            total = None
            for k in range(GROUP):
                left = fit_cols[s * GROUP + k]
                both = mm(left, hi[k * rows:(k + 1) * rows])
                term = both[:q1] + (both[q1:] + mm(left[:q1], lo[k * rows:(k + 1) * rows]))
                total = term if total is None else total + term
            if s == 0:
                dst_sum[:, wide] = total
            else:
                dst_sum[:, wide] += total
        both = mm(hi_all[...], dst_rows[...])
        through = both[:, :q1] + (both[:, q1:] + mm(lo_all[...], dst_rows[:, :q1]))
        for i in range(GROUP):
            k = s * GROUP + i
            th = halves(through[i * rows:(i + 1) * rows], 1)
            right = halves(core_hours[k].T, 1)
            both = mm(th, jnp.concatenate([right, right], axis=0))
            both = both[:, :p1] + both[:, p1:]
            src_sum = both if src_sum is None else src_sum + both
            both = mm(src_cols, th)
            both = both[:p1] + both[p1:]
            projected[k] = both[:, :q1] + both[:, q1:]
    turned[...] = dst_sum[...].T.reshape(turned.shape)
    src_all[...] = src_sum.reshape(src_all.shape)
    first = 3 + steps
    moves = [(turned.at[lax.rem(x + s, X)], out) for s, out in enumerate((a0, a1, a2, a3))]
    half = hours // CORES
    for mine, out in ((c, own), (1 - c, send)):
        moves.append((projected.at[pl.ds(mine * half, half)], out.at[pl.ds(0, half)]))
        moves.append((src_all.at[pl.ds(mine, 1)], out.at[pl.ds(half, 1)]))
    copies = [pltpu.make_async_copy(a, b, sems.at[first + i]) for i, (a, b) in enumerate(moves)]
    for copy in copies:
        copy.start()
    for copy in copies:
        copy.wait()


def main_call(hour, counts, src, dst, core):
    hours, rows, cols = counts.shape
    rank, p1, q1 = core.shape
    block = cols // X
    half = hours // CORES + 1
    return pl.pallas_call(
        main_kernel,
        out_shape=[struct(block, q1)] * X + [struct(half, p1, q1)] * 2,
        in_specs=[SMEM] + [HBM] * 4,
        out_specs=[HBM] * (X + 2),
        scratch_shapes=[
            pltpu.VMEM(counts.shape, jnp.int32),
            pltpu.VMEM(src.shape, F32),
            pltpu.VMEM(dst.shape, F32),
            pltpu.VMEM(core.shape, F32),
            pltpu.VMEM((hours * rows, 3 * q1), BF16),
            pltpu.VMEM((hours, 2 * q1, rows), BF16),
            pltpu.VMEM((3 * q1, cols), BF16),
            pltpu.VMEM((cols, 2 * q1), BF16),
            pltpu.VMEM((GROUP * rows, cols), BF16),
            pltpu.VMEM((GROUP * rows, cols), BF16),
            pltpu.VMEM((q1, cols), F32),
            pltpu.VMEM((X, block, q1), F32),
            pltpu.VMEM((hours, p1, q1), F32),
            pltpu.VMEM((hours, p1, q1), F32),
            pltpu.VMEM((CORES, rows // CORES, p1), F32),
            pltpu.SemaphoreType.DMA((3 + hours // GROUP + X + 4,)),
        ],
        compiler_params=params(60),
        cost_estimate=cost(2 * 9 * counts.size * q1, 14 << 20),
        name="all_terms",
    )(hour, counts, src, dst, core)


def share_kernel(zs, own, came, core, m0, m1, m2, m3, src_half, rowsums, message):
    half = own.shape[0] - 1
    rank, p1, q1 = core.shape
    x = lax.axis_index("x")
    src_half[...] = own[half] + came[half]
    for k in range(half):
        here = own[k] + came[k]
        for r in range(rank):
            product = (here * core[r]).reshape(p1 // 8, 8, q1)
            at = k * rank + r
            rowsums[at:at + 1, :] = jnp.sum(jnp.sum(product, axis=0), axis=0, keepdims=True)
        for z in range(zs):
            for b in range(X):
                start = (z * X + b) * 4
                row = (z * half + k) * 4
                message[b, row:row + 4, :] = here[start:start + 4]
    sums = jnp.sum(rowsums[...].T, axis=0, keepdims=True)
    tail = jnp.concatenate([sums, jnp.zeros((7, q1), F32)], axis=0)
    size = message.shape[1]
    for s, out in enumerate((m0, m1, m2, m3)):
        out[:size, :] = message[lax.rem(x + s, X)]
        out[size:, :] = tail


def share_call(own, came, core, zs):
    half = own.shape[0] - 1
    rank, p1, q1 = core.shape
    size = half * p1 // X
    return pl.pallas_call(
        functools.partial(share_kernel, zs),
        out_shape=[struct(size + 8, q1)] * X + [struct(p1, q1)],
        in_specs=[VMEM] * 3,
        out_specs=[VMEM] * (X + 1),
        scratch_shapes=[pltpu.VMEM((half * rank, q1), F32), pltpu.VMEM((X, size, q1), F32)],
        compiler_params=params(8),
        cost_estimate=cost(1 << 34, 4 << 20),
        name="hour_terms",
    )(own, came, core)


def small_call(kernel, name, outs, args, flops=1 << 20):
    return pl.pallas_call(
        kernel, out_shape=outs, in_specs=[VMEM] * len(args), out_specs=jax.tree.map(lambda _: VMEM, outs),
        compiler_params=params(4), cost_estimate=cost(flops, 1 << 20), name=name,
    )(*args)


def sum_kernel(*refs):
    parts = [ref[...] for ref in refs[:-1]]
    while len(parts) > 1:
        half = len(parts) // 2
        parts = [a + b for a, b in zip(parts[:half], parts[half:])]
    refs[-1][...] = parts[0]


def summed(name, *parts):
    return small_call(sum_kernel, name, struct(*parts[0].shape), parts)


def x_kernel(a0, a1, a2, a3, m0, m1, m2, m3, out):
    zs, rows, _ = out.shape
    share = a0.shape[0] // zs
    each = rows - share - 8
    a = (a0[...] + a2[...]) + (a1[...] + a3[...])
    m = (m0[...] + m2[...]) + (m1[...] + m3[...])
    for z in range(zs):
        out[z, :share, :] = a[z * share:(z + 1) * share]
        out[z, share:share + each, :] = m[z * each:(z + 1) * each]
        out[z, share + each:, :] = m[zs * each:]


def tail_kernel(share, w, src_half, out):
    tail = w.shape[1] - share
    out[:tail, :] = jnp.sum(w[:, share:, :], axis=0)
    out[tail:, :] = src_half[...]


def pair_kernel(own, other, tails, src_both):
    c = lax.axis_index("core")
    tail = tails.shape[1]
    for at, part in ((c, own), (1 - c, other)):
        tails[at] = part[:tail, :]
        src_both[at] = part[tail:, :]


def join_kernel(own, came, src_both, out):
    tail = own.shape[1]
    out[:, :tail, :] = own[...] + came[...]
    out[:, tail:, :] = src_both[...]


def z_kernel(w, copies):
    share = copies.shape[1]
    total = jnp.sum(w[:, :share, :], axis=0)
    for z in range(copies.shape[0]):
        copies[z] = total


def end_kernel(scales, hour_ref, b0, b1, b2, b3, joined, more,
               src_out, dst_out, hour_out, core_out, both):
    x = lax.axis_index("x")
    src_scale, dst_scale, hour_scale, core_scale = scales
    for s, block in enumerate((b0, b1, b2, b3)):
        dst_out[lax.rem(x - s + X, X)] = block[...] * dst_scale
    tail = both.shape[1]
    src_out[...] = (joined[:, tail:, :] + more[:, tail:, :]) * src_scale
    both[...] = joined[:, :tail, :] + more[:, :tail, :]
    hours, rank = hour_ref.shape
    half = hours // CORES
    tiles = []
    for k in range(hours):
        at, i = k // half, k % half
        hour_out[k:k + 1, :] = both[at, 4 * half:4 * half + 1, i * rank:(i + 1) * rank] * hour_scale
        tiles.append(both[at, 4 * i:4 * i + 4, :] * core_scale)
    for r in range(rank):
        out = hour_ref[0, r] * tiles[0]
        for k in range(1, hours):
            out = out + hour_ref[k, r] * tiles[k]
        core_out[r] = out


def end_call(scales, hour, blocks, joined, more):
    block, q1 = blocks[0].shape
    hours, rank = hour.shape
    tail = 4 * hours // CORES + 8
    return pl.pallas_call(
        functools.partial(end_kernel, scales),
        in_specs=[SMEM] + [VMEM] * 6,
        out_specs=[VMEM] * 4,
        out_shape=[struct(CORES, joined.shape[1] - tail, q1), struct(X, block, q1),
                   struct(hours, rank), struct(rank, 4, q1)],
        scratch_shapes=[pltpu.VMEM((CORES, tail, q1), F32)],
        compiler_params=params(8), cost_estimate=cost(1 << 20, 1 << 20), name="outputs",
    )(hour, *blocks, joined, more)


def shifted(x, axis, s):
    n = lax.axis_size(axis)
    return lax.ppermute(x, axis, [(i, (i + s) % n) for i in range(n)])


def swapped(x, axis):
    return lax.all_to_all(x, axis, split_axis=0, concat_axis=0, tiled=True)


def paired(x, axis, flip):
    n = lax.axis_size(axis)
    return lax.ppermute(x, axis, [(i, flip(i, n)) for i in range(n)])


def near(i, n):
    return i ^ 1


def far(i, n):
    return n - 1 - i


def around(x, axis):
    return [x] + [shifted(x, axis, s) for s in range(1, lax.axis_size(axis))]


def shards(scales, counts, src_factor, dst_factor, hour_factor, core):
    zs = lax.axis_size("z")
    q1 = dst_factor.shape[1]
    a0, a1, a2, a3, own, send = main_call(hour_factor, counts, src_factor, dst_factor, core)
    a = [a0] + [shifted(v, "x", s) for s, v in ((1, a1), (2, a2), (3, a3))]
    m0, m1, m2, m3, src_half = share_call(own, shifted(send, "core", 1), core, zs)
    m = [m0] + [shifted(v, "x", s) for s, v in ((1, m1), (2, m2), (3, m3))]
    share = a0.shape[0] // zs
    each = (m0.shape[0] - 8) // zs
    src_half, a[1], a[2] = lax.optimization_barrier((src_half, a[1], a[2]))
    src_half = summed("src_near_sum", src_half, paired(src_half, "y", near))
    m, src_half = lax.optimization_barrier((m, src_half))
    w = small_call(x_kernel, "x_sums", struct(zs, share + each + 8, q1), [*a, *m])
    w = swapped(w, "z")
    tail = each + 8
    own = small_call(functools.partial(tail_kernel, share), "tail_sums",
                     struct(tail + src_half.shape[0], q1), [w, src_half])
    copies = small_call(z_kernel, "z_sums", struct(zs, share, q1), [w])
    tails, src_both = small_call(pair_kernel, "both_tails",
                                 [struct(CORES, tail, q1), struct(CORES, *src_half.shape)],
                                 [own, shifted(own, "core", 1)])
    joined = small_call(join_kernel, "near_sum", struct(CORES, *own.shape),
                        [tails, paired(tails, "y", near), src_both])
    block = swapped(copies, "z").reshape(zs * share, q1)
    block, joined = lax.optimization_barrier((block, joined))
    more = paired(joined, "y", far)
    blocks = around(block, "x")
    grad_src, grad_dst, grad_hour, grad_core = end_call(
        scales, hour_factor, blocks, joined, more)
    return (grad_src.reshape(src_factor.shape), grad_dst.reshape(dst_factor.shape), grad_hour, grad_core)


def solution(mesh):
    n_src, n_dst = mesh.shape["src"], mesh.shape["dst"]
    fine = Mesh(mesh.devices.reshape(n_src // X, X, n_dst // CORES, CORES), ("z", "x", "y", "core"))
    src, dst = ("z", "x"), ("y", "core")
    in_specs = (P(None, src, dst), P(src, None), P(dst, None), P(), P())
    out_specs = (P(src, None), P(dst, None), P(), P(None, src, None))

    def run(counts, src_factor, dst_factor, hour_factor, core):
        hours, total_src, total_dst = counts.shape
        scales = (1 / math.sqrt(total_dst * hours), 1 / math.sqrt(total_src * hours),
                  1 / math.sqrt(total_src * total_dst), 1 / math.sqrt(total_src * total_dst * hours))
        body = jax.shard_map(functools.partial(shards, scales), mesh=fine, in_specs=in_specs,
                             out_specs=out_specs, check_vma=False)
        return body(counts, src_factor, dst_factor, hour_factor, core)

    return run
```

```python
import functools
import math

import jax
import jax.numpy as jnp
from jax import lax
from jax.experimental import pallas as pl
from jax.experimental.pallas import tpu as pltpu
from jax.sharding import Mesh, PartitionSpec as P

X = 4
CORES = 2
GROUP = 4
SPAN = 512
F32 = jnp.float32
BF16 = jnp.bfloat16
HBM = pl.BlockSpec(memory_space=pltpu.HBM)
VMEM = pl.BlockSpec(memory_space=pltpu.VMEM)
SMEM = pl.BlockSpec(memory_space=pltpu.SMEM)


def struct(*shape, dtype=F32):
    return jax.ShapeDtypeStruct(shape, dtype)


def params(mib):
    return pltpu.CompilerParams(vmem_limit_bytes=mib << 20)


def cost(flops, size):
    return pl.CostEstimate(flops=flops, bytes_accessed=size, transcendentals=0)


def split(x):
    hi = x.astype(BF16)
    return hi, (x - hi.astype(F32)).astype(BF16)


def mm(a, b):
    return jnp.dot(a, b, preferred_element_type=F32)


def halves(x, axis):
    return jnp.concatenate(split(x), axis=axis)


def main_kernel(hour_ref, counts_hbm, src_hbm, dst_hbm, core_hbm,
                a0, a1, a2, a3, own, send,
                counts, src, dst, core, fit_rows, fit_cols, dst_cols, dst_rows, hi_all, lo_all, dst_sum, turned,
                core_hours, projected, src_all, sems):
    hours, rows, cols = counts.shape
    rank, p1, q1 = core.shape
    steps = hours // GROUP
    x, c = lax.axis_index("x"), lax.axis_index("core")
    small = [pltpu.make_async_copy(a, b, sems.at[i])
             for i, (a, b) in enumerate(((core_hbm, core), (src_hbm, src), (dst_hbm, dst)))]
    parts = [pl.ds(s * GROUP, GROUP) for s in range(steps)]
    large = [pltpu.make_async_copy(counts_hbm.at[part], counts.at[part], sems.at[3 + s])
             for s, part in enumerate(parts)]
    for copy in small[::-1] + large:
        copy.start()
    small[2].wait()
    dst_rows[...] = halves(dst[...], 1)
    hi, lo = split(dst[...].T)
    dst_cols[...] = jnp.concatenate([hi, hi, lo], axis=0)
    small[0].wait()
    small[1].wait()
    hi, lo = split(src[...])
    src_rows = jnp.concatenate([hi, lo, hi], axis=1)
    for k in range(hours):
        core_hour = hour_ref[k, 0] * core[0]
        for r in range(1, rank):
            core_hour = core_hour + hour_ref[k, r] * core[r]
        core_hours[k] = core_hour
        hi, lo = split(core_hour)
        fit = mm(src_rows, jnp.concatenate([hi, hi, lo], axis=0))
        hi, lo = split(fit)
        fit_rows[k * rows:(k + 1) * rows] = jnp.concatenate([hi, lo, hi], axis=1)
        fit_cols[k] = halves(fit.T, 0)
    src_cols = halves(src[...].T, 0)
    src_sum = None
    for s, part in enumerate(parts):
        large[s].wait()
        for j in range(0, cols, SPAN):
            wide = pl.ds(j, SPAN)
            fitted = mm(fit_rows[s * GROUP * rows:(s + 1) * GROUP * rows, :], dst_cols[:, wide])
            misfit = 1.0 - counts[part, :, wide].reshape(GROUP * rows, SPAN).astype(F32) / fitted
            hi, lo = split(misfit)
            hi_all[:, wide] = hi
            lo_all[:, wide] = lo
            total = None
            for k in range(GROUP):
                left = fit_cols[s * GROUP + k]
                both = mm(left, hi[k * rows:(k + 1) * rows])
                term = both[:q1] + (both[q1:] + mm(left[:q1], lo[k * rows:(k + 1) * rows]))
                total = term if total is None else total + term
            if s == 0:
                dst_sum[:, wide] = total
            else:
                dst_sum[:, wide] += total
        both = mm(hi_all[...], dst_rows[...])
        through = both[:, :q1] + (both[:, q1:] + mm(lo_all[...], dst_rows[:, :q1]))
        for i in range(GROUP):
            k = s * GROUP + i
            th = halves(through[i * rows:(i + 1) * rows], 1)
            right = halves(core_hours[k].T, 1)
            both = mm(th, jnp.concatenate([right, right], axis=0))
            both = both[:, :p1] + both[:, p1:]
            src_sum = both if src_sum is None else src_sum + both
            both = mm(src_cols, th)
            both = both[:p1] + both[p1:]
            projected[k] = both[:, :q1] + both[:, q1:]
    turned[...] = dst_sum[...].T.reshape(turned.shape)
    src_all[...] = src_sum.reshape(src_all.shape)
    first = 3 + steps
    moves = [(turned.at[lax.rem(x + s, X)], out) for s, out in enumerate((a0, a1, a2, a3))]
    half = hours // CORES
    for mine, out in ((c, own), (1 - c, send)):
        moves.append((projected.at[pl.ds(mine * half, half)], out.at[pl.ds(0, half)]))
        moves.append((src_all.at[pl.ds(mine, 1)], out.at[pl.ds(half, 1)]))
    copies = [pltpu.make_async_copy(a, b, sems.at[first + i]) for i, (a, b) in enumerate(moves)]
    for copy in copies:
        copy.start()
    for copy in copies:
        copy.wait()


def main_call(hour, counts, src, dst, core):
    hours, rows, cols = counts.shape
    rank, p1, q1 = core.shape
    block = cols // X
    half = hours // CORES + 1
    return pl.pallas_call(
        main_kernel,
        out_shape=[struct(block, q1)] * X + [struct(half, p1, q1)] * 2,
        in_specs=[SMEM] + [HBM] * 4,
        out_specs=[HBM] * (X + 2),
        scratch_shapes=[
            pltpu.VMEM(counts.shape, jnp.int32),
            pltpu.VMEM(src.shape, F32),
            pltpu.VMEM(dst.shape, F32),
            pltpu.VMEM(core.shape, F32),
            pltpu.VMEM((hours * rows, 3 * q1), BF16),
            pltpu.VMEM((hours, 2 * q1, rows), BF16),
            pltpu.VMEM((3 * q1, cols), BF16),
            pltpu.VMEM((cols, 2 * q1), BF16),
            pltpu.VMEM((GROUP * rows, cols), BF16),
            pltpu.VMEM((GROUP * rows, cols), BF16),
            pltpu.VMEM((q1, cols), F32),
            pltpu.VMEM((X, block, q1), F32),
            pltpu.VMEM((hours, p1, q1), F32),
            pltpu.VMEM((hours, p1, q1), F32),
            pltpu.VMEM((CORES, rows // CORES, p1), F32),
            pltpu.SemaphoreType.DMA((3 + hours // GROUP + X + 4,)),
        ],
        compiler_params=params(60),
        cost_estimate=cost(2 * 9 * counts.size * q1, 14 << 20),
        name="all_terms",
    )(hour, counts, src, dst, core)


def share_kernel(zs, own, came, core, m0, m1, m2, m3, src_half, rowsums, message):
    half = own.shape[0] - 1
    rank, p1, q1 = core.shape
    x = lax.axis_index("x")
    src_half[...] = own[half] + came[half]
    for k in range(half):
        here = own[k] + came[k]
        for r in range(rank):
            product = (here * core[r]).reshape(p1 // 8, 8, q1)
            at = k * rank + r
            rowsums[at:at + 1, :] = jnp.sum(jnp.sum(product, axis=0), axis=0, keepdims=True)
        for z in range(zs):
            for b in range(X):
                start = (z * X + b) * 4
                row = (z * half + k) * 4
                message[b, row:row + 4, :] = here[start:start + 4]
    sums = jnp.sum(rowsums[...].T, axis=0, keepdims=True)
    tail = jnp.concatenate([sums, jnp.zeros((7, q1), F32)], axis=0)
    size = message.shape[1]
    for s, out in enumerate((m0, m1, m2, m3)):
        out[:size, :] = message[lax.rem(x + s, X)]
        out[size:, :] = tail


def share_call(own, came, core, zs):
    half = own.shape[0] - 1
    rank, p1, q1 = core.shape
    size = half * p1 // X
    return pl.pallas_call(
        functools.partial(share_kernel, zs),
        out_shape=[struct(size + 8, q1)] * X + [struct(p1, q1)],
        in_specs=[VMEM] * 3,
        out_specs=[VMEM] * (X + 1),
        scratch_shapes=[pltpu.VMEM((half * rank, q1), F32), pltpu.VMEM((X, size, q1), F32)],
        compiler_params=params(8),
        cost_estimate=cost(1 << 34, 4 << 20),
        name="hour_terms",
    )(own, came, core)


def small_call(kernel, name, outs, args, flops=1 << 20):
    return pl.pallas_call(
        kernel, out_shape=outs, in_specs=[VMEM] * len(args), out_specs=jax.tree.map(lambda _: VMEM, outs),
        compiler_params=params(4), cost_estimate=cost(flops, 1 << 20), name=name,
    )(*args)


def sum_kernel(*refs):
    parts = [ref[...] for ref in refs[:-1]]
    while len(parts) > 1:
        half = len(parts) // 2
        parts = [a + b for a, b in zip(parts[:half], parts[half:])]
    refs[-1][...] = parts[0]


def summed(name, *parts):
    return small_call(sum_kernel, name, struct(*parts[0].shape), parts)


def x_kernel(a0, a1, a2, a3, m0, m1, m2, m3, out):
    zs, rows, _ = out.shape
    share = a0.shape[0] // zs
    each = rows - share - 8
    a = (a0[...] + a2[...]) + (a1[...] + a3[...])
    m = (m0[...] + m2[...]) + (m1[...] + m3[...])
    for z in range(zs):
        out[z, :share, :] = a[z * share:(z + 1) * share]
        out[z, share:share + each, :] = m[z * each:(z + 1) * each]
        out[z, share + each:, :] = m[zs * each:]


def tail_kernel(share, w, src_half, out):
    tail = w.shape[1] - share
    out[:tail, :] = jnp.sum(w[:, share:, :], axis=0)
    out[tail:, :] = src_half[...]


def z_kernel(w, copies):
    share = copies.shape[1]
    total = jnp.sum(w[:, :share, :], axis=0)
    for z in range(copies.shape[0]):
        copies[z] = total


def end_kernel(scales, hour_ref, b0, b1, b2, b3, own, distant, sibling, diagonal,
               src_out, dst_out, hour_out, core_out, both):
    x, c = lax.axis_index("x"), lax.axis_index("core")
    src_scale, dst_scale, hour_scale, core_scale = scales
    for s, block in enumerate((b0, b1, b2, b3)):
        dst_out[lax.rem(x - s + X, X)] = block[...] * dst_scale
    tail = both.shape[1]
    for at, p, q in ((c, own, distant), (1 - c, sibling, diagonal)):
        total = p[...] + q[...]
        both[at] = total[:tail]
        src_out[at] = total[tail:] * src_scale
    hours, rank = hour_ref.shape
    half = hours // CORES
    tiles = []
    for k in range(hours):
        at, i = k // half, k % half
        hour_out[k:k + 1, :] = both[at, 4 * half:4 * half + 1, i * rank:(i + 1) * rank] * hour_scale
        tiles.append(both[at, 4 * i:4 * i + 4, :] * core_scale)
    for r in range(rank):
        out = hour_ref[0, r] * tiles[0]
        for k in range(1, hours):
            out = out + hour_ref[k, r] * tiles[k]
        core_out[r] = out


def end_call(scales, hour, blocks, sums):
    block, q1 = blocks[0].shape
    hours, rank = hour.shape
    tail = 4 * hours // CORES + 8
    return pl.pallas_call(
        functools.partial(end_kernel, scales),
        in_specs=[SMEM] + [VMEM] * 8,
        out_specs=[VMEM] * 4,
        out_shape=[struct(CORES, sums[0].shape[0] - tail, q1), struct(X, block, q1),
                   struct(hours, rank), struct(rank, 4, q1)],
        scratch_shapes=[pltpu.VMEM((CORES, tail, q1), F32)],
        compiler_params=params(8), cost_estimate=cost(1 << 20, 1 << 20), name="outputs",
    )(hour, *blocks, *sums)


def shifted(x, axis, s):
    n = lax.axis_size(axis)
    return lax.ppermute(x, axis, [(i, (i + s) % n) for i in range(n)])


def swapped(x, axis):
    return lax.all_to_all(x, axis, split_axis=0, concat_axis=0, tiled=True)


def paired(x, axis, flip):
    n = lax.axis_size(axis)
    return lax.ppermute(x, axis, [(i, flip(i, n)) for i in range(n)])


def near(i, n):
    return i ^ 1


def far(i, n):
    return n - 1 - i


def around(x, axis):
    return [x] + [shifted(x, axis, s) for s in range(1, lax.axis_size(axis))]


def shards(scales, counts, src_factor, dst_factor, hour_factor, core):
    zs = lax.axis_size("z")
    q1 = dst_factor.shape[1]
    a0, a1, a2, a3, own, send = main_call(hour_factor, counts, src_factor, dst_factor, core)
    a = [a0] + [shifted(v, "x", s) for s, v in ((1, a1), (2, a2), (3, a3))]
    m0, m1, m2, m3, src_half = share_call(own, shifted(send, "core", 1), core, zs)
    m = [m0] + [shifted(v, "x", s) for s, v in ((1, m1), (2, m2), (3, m3))]
    share = a0.shape[0] // zs
    each = (m0.shape[0] - 8) // zs
    w = small_call(x_kernel, "x_sums", struct(zs, share + each + 8, q1), [*a, *m])
    w = swapped(w, "z")
    tail = each + 8
    own = small_call(functools.partial(tail_kernel, share), "tail_sums",
                     struct(tail + src_half.shape[0], q1), [w, src_half])
    copies = small_call(z_kernel, "z_sums", struct(zs, share, q1), [w])
    own = summed("near_sum", own, paired(own, "y", near))
    block = swapped(copies, "z").reshape(zs * share, q1)
    block, own = lax.optimization_barrier((block, own))
    mine = [own, paired(own, "y", far)]
    others = [shifted(own, "core", 1), paired(own, ("y", "core"), far)]
    blocks = around(block, "x")
    grad_src, grad_dst, grad_hour, grad_core = end_call(
        scales, hour_factor, blocks, mine + others)
    return (grad_src.reshape(src_factor.shape), grad_dst.reshape(dst_factor.shape), grad_hour, grad_core)


def solution(mesh):
    n_src, n_dst = mesh.shape["src"], mesh.shape["dst"]
    fine = Mesh(mesh.devices.reshape(n_src // X, X, n_dst // CORES, CORES), ("z", "x", "y", "core"))
    src, dst = ("z", "x"), ("y", "core")
    in_specs = (P(None, src, dst), P(src, None), P(dst, None), P(), P())
    out_specs = (P(src, None), P(dst, None), P(), P(None, src, None))

    def run(counts, src_factor, dst_factor, hour_factor, core):
        hours, total_src, total_dst = counts.shape
        scales = (1 / math.sqrt(total_dst * hours), 1 / math.sqrt(total_src * hours),
                  1 / math.sqrt(total_src * total_dst), 1 / math.sqrt(total_src * total_dst * hours))
        body = jax.shard_map(functools.partial(shards, scales), mesh=fine, in_specs=in_specs,
                             out_specs=out_specs, check_vma=False)
        return body(counts, src_factor, dst_factor, hour_factor, core)

    return run
```

```python
import functools
import math

import jax
import jax.numpy as jnp
from jax import lax
from jax.experimental import pallas as pl
from jax.experimental.pallas import tpu as pltpu
from jax.sharding import Mesh, PartitionSpec as P

X = 4
CORES = 2
GROUP = 4
SPAN = 512
F32 = jnp.float32
BF16 = jnp.bfloat16
HBM = pl.BlockSpec(memory_space=pltpu.HBM)
VMEM = pl.BlockSpec(memory_space=pltpu.VMEM)
SMEM = pl.BlockSpec(memory_space=pltpu.SMEM)


def struct(*shape, dtype=F32):
    return jax.ShapeDtypeStruct(shape, dtype)


def params(mib):
    return pltpu.CompilerParams(vmem_limit_bytes=mib << 20)


def cost(flops, size):
    return pl.CostEstimate(flops=flops, bytes_accessed=size, transcendentals=0)


def split(x):
    hi = x.astype(BF16)
    return hi, (x - hi.astype(F32)).astype(BF16)


def mm(a, b):
    return jnp.dot(a, b, preferred_element_type=F32)


def halves(x, axis):
    return jnp.concatenate(split(x), axis=axis)


def main_kernel(hour_ref, counts_hbm, src_hbm, dst_hbm, core_hbm,
                a0, a1, a2, a3, own, send,
                counts, src, dst, core, fit_rows, fit_cols, dst_cols, dst_rows, hi_all, lo_all, dst_sum, turned,
                core_hours, projected, src_all, sems):
    hours, rows, cols = counts.shape
    rank, p1, q1 = core.shape
    steps = hours // GROUP
    x, c = lax.axis_index("x"), lax.axis_index("core")
    small = [pltpu.make_async_copy(a, b, sems.at[i])
             for i, (a, b) in enumerate(((core_hbm, core), (src_hbm, src), (dst_hbm, dst)))]
    parts = [pl.ds(s * GROUP, GROUP) for s in range(steps)]
    large = [pltpu.make_async_copy(counts_hbm.at[part], counts.at[part], sems.at[3 + s])
             for s, part in enumerate(parts)]
    for copy in small[::-1] + large:
        copy.start()
    small[2].wait()
    dst_rows[...] = halves(dst[...], 1)
    hi, lo = split(dst[...].T)
    dst_cols[...] = jnp.concatenate([hi, hi, lo], axis=0)
    small[0].wait()
    small[1].wait()
    hi, lo = split(src[...])
    src_rows = jnp.concatenate([hi, lo, hi], axis=1)
    for k in range(hours):
        core_hour = hour_ref[k, 0] * core[0]
        for r in range(1, rank):
            core_hour = core_hour + hour_ref[k, r] * core[r]
        core_hours[k] = core_hour
        hi, lo = split(core_hour)
        fit = mm(src_rows, jnp.concatenate([hi, hi, lo], axis=0))
        hi, lo = split(fit)
        fit_rows[k * rows:(k + 1) * rows] = jnp.concatenate([hi, lo, hi], axis=1)
        fit_cols[k] = halves(fit.T, 0)
    src_cols = halves(src[...].T, 0)
    src_sum = None
    for s, part in enumerate(parts):
        large[s].wait()
        for j in range(0, cols, SPAN):
            wide = pl.ds(j, SPAN)
            fitted = mm(fit_rows[s * GROUP * rows:(s + 1) * GROUP * rows, :], dst_cols[:, wide])
            misfit = 1.0 - counts[part, :, wide].reshape(GROUP * rows, SPAN).astype(F32) / fitted
            hi, lo = split(misfit)
            hi_all[:, wide] = hi
            lo_all[:, wide] = lo
            total = None
            for k in range(GROUP):
                left = fit_cols[s * GROUP + k]
                both = mm(left, hi[k * rows:(k + 1) * rows])
                term = both[:q1] + (both[q1:] + mm(left[:q1], lo[k * rows:(k + 1) * rows]))
                total = term if total is None else total + term
            if s == 0:
                dst_sum[:, wide] = total
            else:
                dst_sum[:, wide] += total
        both = mm(hi_all[...], dst_rows[...])
        through = both[:, :q1] + (both[:, q1:] + mm(lo_all[...], dst_rows[:, :q1]))
        for i in range(GROUP):
            k = s * GROUP + i
            th = halves(through[i * rows:(i + 1) * rows], 1)
            right = halves(core_hours[k].T, 1)
            both = mm(th, jnp.concatenate([right, right], axis=0))
            both = both[:, :p1] + both[:, p1:]
            src_sum = both if src_sum is None else src_sum + both
            both = mm(src_cols, th)
            both = both[:p1] + both[p1:]
            projected[k] = both[:, :q1] + both[:, q1:]
    turned[...] = dst_sum[...].T.reshape(turned.shape)
    src_all[...] = src_sum.reshape(src_all.shape)
    first = 3 + steps
    moves = [(turned.at[lax.rem(x + s, X)], out) for s, out in enumerate((a0, a1, a2, a3))]
    half = hours // CORES
    for mine, out in ((c, own), (1 - c, send)):
        moves.append((projected.at[pl.ds(mine * half, half)], out.at[pl.ds(0, half)]))
        moves.append((src_all.at[pl.ds(mine, 1)], out.at[pl.ds(half, 1)]))
    copies = [pltpu.make_async_copy(a, b, sems.at[first + i]) for i, (a, b) in enumerate(moves)]
    for copy in copies:
        copy.start()
    for copy in copies:
        copy.wait()


def main_call(hour, counts, src, dst, core):
    hours, rows, cols = counts.shape
    rank, p1, q1 = core.shape
    block = cols // X
    half = hours // CORES + 1
    return pl.pallas_call(
        main_kernel,
        out_shape=[struct(block, q1)] * X + [struct(half, p1, q1)] * 2,
        in_specs=[SMEM] + [HBM] * 4,
        out_specs=[HBM] * (X + 2),
        scratch_shapes=[
            pltpu.VMEM(counts.shape, jnp.int32),
            pltpu.VMEM(src.shape, F32),
            pltpu.VMEM(dst.shape, F32),
            pltpu.VMEM(core.shape, F32),
            pltpu.VMEM((hours * rows, 3 * q1), BF16),
            pltpu.VMEM((hours, 2 * q1, rows), BF16),
            pltpu.VMEM((3 * q1, cols), BF16),
            pltpu.VMEM((cols, 2 * q1), BF16),
            pltpu.VMEM((GROUP * rows, cols), BF16),
            pltpu.VMEM((GROUP * rows, cols), BF16),
            pltpu.VMEM((q1, cols), F32),
            pltpu.VMEM((X, block, q1), F32),
            pltpu.VMEM((hours, p1, q1), F32),
            pltpu.VMEM((hours, p1, q1), F32),
            pltpu.VMEM((CORES, rows // CORES, p1), F32),
            pltpu.SemaphoreType.DMA((3 + hours // GROUP + X + 4,)),
        ],
        compiler_params=params(60),
        cost_estimate=cost(2 * 9 * counts.size * q1, 14 << 20),
        name="all_terms",
    )(hour, counts, src, dst, core)


def share_kernel(zs, own, came, core, m0, m1, m2, m3, src_half, rowsums, message):
    half = own.shape[0] - 1
    rank, p1, q1 = core.shape
    x = lax.axis_index("x")
    src_half[...] = own[half] + came[half]
    for k in range(half):
        here = own[k] + came[k]
        for r in range(rank):
            product = (here * core[r]).reshape(p1 // 8, 8, q1)
            at = k * rank + r
            rowsums[at:at + 1, :] = jnp.sum(jnp.sum(product, axis=0), axis=0, keepdims=True)
        for z in range(zs):
            for b in range(X):
                start = (z * X + b) * 4
                row = (z * half + k) * 4
                message[b, row:row + 4, :] = here[start:start + 4]
    sums = jnp.sum(rowsums[...].T, axis=0, keepdims=True)
    tail = jnp.concatenate([sums, jnp.zeros((7, q1), F32)], axis=0)
    size = message.shape[1]
    for s, out in enumerate((m0, m1, m2, m3)):
        out[:size, :] = message[lax.rem(x + s, X)]
        out[size:, :] = tail


def share_call(own, came, core, zs):
    half = own.shape[0] - 1
    rank, p1, q1 = core.shape
    size = half * p1 // X
    return pl.pallas_call(
        functools.partial(share_kernel, zs),
        out_shape=[struct(size + 8, q1)] * X + [struct(p1, q1)],
        in_specs=[VMEM] * 3,
        out_specs=[VMEM] * (X + 1),
        scratch_shapes=[pltpu.VMEM((half * rank, q1), F32), pltpu.VMEM((X, size, q1), F32)],
        compiler_params=params(8),
        cost_estimate=cost(1 << 34, 4 << 20),
        name="hour_terms",
    )(own, came, core)


def small_call(kernel, name, outs, args, flops=1 << 20):
    return pl.pallas_call(
        kernel, out_shape=outs, in_specs=[VMEM] * len(args), out_specs=jax.tree.map(lambda _: VMEM, outs),
        compiler_params=params(4), cost_estimate=cost(flops, 1 << 20), name=name,
    )(*args)


def sum_kernel(*refs):
    parts = [ref[...] for ref in refs[:-1]]
    while len(parts) > 1:
        half = len(parts) // 2
        parts = [a + b for a, b in zip(parts[:half], parts[half:])]
    refs[-1][...] = parts[0]


def summed(name, *parts):
    return small_call(sum_kernel, name, struct(*parts[0].shape), parts)


def x_kernel(a0, a1, a2, a3, m0, m1, m2, m3, out):
    zs, rows, _ = out.shape
    share = a0.shape[0] // zs
    each = rows - share - 8
    a = (a0[...] + a2[...]) + (a1[...] + a3[...])
    m = (m0[...] + m2[...]) + (m1[...] + m3[...])
    for z in range(zs):
        out[z, :share, :] = a[z * share:(z + 1) * share]
        out[z, share:share + each, :] = m[z * each:(z + 1) * each]
        out[z, share + each:, :] = m[zs * each:]


def tail_kernel(share, w, src_half, out):
    tail = w.shape[1] - share
    out[:tail, :] = jnp.sum(w[:, share:, :], axis=0)
    out[tail:, :] = src_half[...]


def pair_kernel(own, other, out):
    c = lax.axis_index("core")
    out[c] = own[...]
    out[1 - c] = other[...]


def z_kernel(w, copies):
    share = copies.shape[1]
    total = jnp.sum(w[:, :share, :], axis=0)
    for z in range(copies.shape[0]):
        copies[z] = total


def end_kernel(scales, hour_ref, b0, b1, b2, b3, joined, more,
               src_out, dst_out, hour_out, core_out, both):
    x = lax.axis_index("x")
    src_scale, dst_scale, hour_scale, core_scale = scales
    for s, block in enumerate((b0, b1, b2, b3)):
        dst_out[lax.rem(x - s + X, X)] = block[...] * dst_scale
    tail = both.shape[1]
    src_out[...] = (joined[:, tail:, :] + more[:, tail:, :]) * src_scale
    both[...] = joined[:, :tail, :] + more[:, :tail, :]
    hours, rank = hour_ref.shape
    half = hours // CORES
    tiles = []
    for k in range(hours):
        at, i = k // half, k % half
        hour_out[k:k + 1, :] = both[at, 4 * half:4 * half + 1, i * rank:(i + 1) * rank] * hour_scale
        tiles.append(both[at, 4 * i:4 * i + 4, :] * core_scale)
    for r in range(rank):
        out = hour_ref[0, r] * tiles[0]
        for k in range(1, hours):
            out = out + hour_ref[k, r] * tiles[k]
        core_out[r] = out


def end_call(scales, hour, blocks, sums):
    block, q1 = blocks[0].shape
    hours, rank = hour.shape
    tail = 4 * hours // CORES + 8
    return pl.pallas_call(
        functools.partial(end_kernel, scales),
        in_specs=[SMEM] + [VMEM] * 6,
        out_specs=[VMEM] * 4,
        out_shape=[struct(CORES, sums[0].shape[1] - tail, q1), struct(X, block, q1),
                   struct(hours, rank), struct(rank, 4, q1)],
        scratch_shapes=[pltpu.VMEM((CORES, tail, q1), F32)],
        compiler_params=params(8), cost_estimate=cost(1 << 20, 1 << 20), name="outputs",
    )(hour, *blocks, *sums)


def shifted(x, axis, s):
    n = lax.axis_size(axis)
    return lax.ppermute(x, axis, [(i, (i + s) % n) for i in range(n)])


def swapped(x, axis):
    return lax.all_to_all(x, axis, split_axis=0, concat_axis=0, tiled=True)


def paired(x, axis, flip):
    n = lax.axis_size(axis)
    return lax.ppermute(x, axis, [(i, flip(i, n)) for i in range(n)])


def near(i, n):
    return i ^ 1


def far(i, n):
    return n - 1 - i


def around(x, axis):
    return [x] + [shifted(x, axis, s) for s in range(1, lax.axis_size(axis))]


def shards(scales, counts, src_factor, dst_factor, hour_factor, core):
    zs = lax.axis_size("z")
    q1 = dst_factor.shape[1]
    a0, a1, a2, a3, own, send = main_call(hour_factor, counts, src_factor, dst_factor, core)
    a = [a0] + [shifted(v, "x", s) for s, v in ((1, a1), (2, a2), (3, a3))]
    m0, m1, m2, m3, src_half = share_call(own, shifted(send, "core", 1), core, zs)
    m = [m0] + [shifted(v, "x", s) for s, v in ((1, m1), (2, m2), (3, m3))]
    share = a0.shape[0] // zs
    each = (m0.shape[0] - 8) // zs
    w = small_call(x_kernel, "x_sums", struct(zs, share + each + 8, q1), [*a, *m])
    w = swapped(w, "z")
    tail = each + 8
    own = small_call(functools.partial(tail_kernel, share), "tail_sums",
                     struct(tail + src_half.shape[0], q1), [w, src_half])
    copies = small_call(z_kernel, "z_sums", struct(zs, share, q1), [w])
    own = summed("near_sum", own, paired(own, "y", near))
    both = small_call(pair_kernel, "both_tails", struct(CORES, *own.shape), [own, shifted(own, "core", 1)])
    block = swapped(copies, "z").reshape(zs * share, q1)
    block, both = lax.optimization_barrier((block, both))
    more = paired(both, "y", far)
    blocks = around(block, "x")
    grad_src, grad_dst, grad_hour, grad_core = end_call(
        scales, hour_factor, blocks, [both, more])
    return (grad_src.reshape(src_factor.shape), grad_dst.reshape(dst_factor.shape), grad_hour, grad_core)


def solution(mesh):
    n_src, n_dst = mesh.shape["src"], mesh.shape["dst"]
    fine = Mesh(mesh.devices.reshape(n_src // X, X, n_dst // CORES, CORES), ("z", "x", "y", "core"))
    src, dst = ("z", "x"), ("y", "core")
    in_specs = (P(None, src, dst), P(src, None), P(dst, None), P(), P())
    out_specs = (P(src, None), P(dst, None), P(), P(None, src, None))

    def run(counts, src_factor, dst_factor, hour_factor, core):
        hours, total_src, total_dst = counts.shape
        scales = (1 / math.sqrt(total_dst * hours), 1 / math.sqrt(total_src * hours),
                  1 / math.sqrt(total_src * total_dst), 1 / math.sqrt(total_src * total_dst * hours))
        body = jax.shard_map(functools.partial(shards, scales), mesh=fine, in_specs=in_specs,
                             out_specs=out_specs, check_vma=False)
        return body(counts, src_factor, dst_factor, hour_factor, core)

    return run
```
